256 devices in a mesh: ctx: 32 (over y, x, core), head: 8 (over z).
Axes of the slice: x: 4, y: 4, z: 8, core: 2. Of those that a mesh axis runs over, the one named last changes fastest.
Arguments:
- query_input: bfloat16 [16384, 4096], P('ctx', 'head'), may hold values from -96 to 96
- key_input: bfloat16 [16384, 4096], P('ctx', 'head'), may hold values from -6 to 6
- value_input: bfloat16 [16384, 4096], P('ctx', 'head'), may hold values from -6 to 6
- out_weight: bfloat16 [4096, 4096], P('head'), may hold values from -0.125 to 0.125
- out_cotangent: bfloat16 [16384, 4096], P('ctx', 'head'), may hold values from -6 to 6
Outputs:
- mixed: float32 [16384, 4096], P('ctx', 'head')
- grad_q: float32 [16384, 4096], P('ctx', 'head')
- grad_k: float32 [16384, 4096], P('ctx', 'head')
- grad_v: float32 [16384, 4096], P('ctx', 'head')
- weight_grad: float32 [4096, 4096], P('head', 'ctx')
- level_max: float32 [5, 32], P(None, 'head')
The draws below stay inside these ranges and needn't reach their ends.
All inputs are finite; a program needn't handle non-finite values.
Results may differ from the reference program's by a relative error of at most 0.04.
Values may be sent and summed in bfloat16 or wider, within the bound.
A program may use at most 128 MiB of HBM per device.

```python
import math
import jax
import jax.numpy as jnp
from jax import lax

D = 4096
H = 32
DH = 128
BLK = 128
LEVELS = 5
TOK_DEV = 512
SEQ = 16384


def rising(length_total, lower_end, upper_end):
    position = jnp.arange(length_total, dtype=jnp.float32) / float(length_total - 1)
    return lower_end + (upper_end - lower_end) * position


def rough_part(key):
    return jnp.clip(jax.random.normal(key, (SEQ, D), jnp.float32), -4.0, 4.0)


def segment_part(key):
    blocks = jnp.clip(jax.random.normal(key, (SEQ // TOK_DEV, D), jnp.float32), -3.0, 3.0)
    return jnp.repeat(blocks, TOK_DEV, axis=0)


def query_key_pair(key):
    streams = jax.random.split(jax.random.fold_in(key, 7), 4)
    growth = rising(SEQ, 1.0, 3.0)
    queries = growth[:, None] * (0.8 * rough_part(streams[0]) + 0.8 * segment_part(streams[1]))
    key_rows = 0.8 * rough_part(streams[2]) + 0.8 * segment_part(streams[3])
    return (queries, key_rows)


def draw_query_input(key, part):
    return query_key_pair(key)[0].astype(jnp.bfloat16)


def draw_key_input(key, part):
    return query_key_pair(key)[1].astype(jnp.bfloat16)


def draw_value_input(key, part):
    streams = jax.random.split(jax.random.fold_in(key, 19), 2)
    values = 0.7 * rough_part(streams[0]) + segment_part(streams[1])
    return values.astype(jnp.bfloat16)


def raised(result, rng, source, target, parts, factor):
    def block_of(dim):
        return (jnp.arange(result.shape[dim]) // (result.shape[dim] // parts)).reshape((-1,) + (1,) * (result.ndim - 1 - dim))

    one_side = jax.random.permutation(rng, parts)[block_of(target)]
    far = (block_of(target) + parts // 2) % parts
    return jnp.where((block_of(source) == one_side) | (block_of(source) == far), factor * result, result)


def shard_levels(own_key, shape, pieces, least, largest):
    level = 1.0
    for dim, shards_of in pieces:
        draws = jax.random.uniform(jax.random.fold_in(jax.random.fold_in(own_key, 6), dim), (shards_of,), jnp.float32, least / len(pieces), largest / len(pieces))
        level = level * jnp.repeat(jnp.exp(draws), shape[dim] // shards_of).reshape((-1,) + (1,) * (len(shape) - 1 - dim))
    return level


def noise_with(stream_key, dims, spread, limit, shards, heavy, kind=jnp.bfloat16):
    array = spread * jax.random.normal(stream_key, dims, jnp.float32)
    if shards:
        array = array * shard_levels(stream_key, dims, shards, -0.22, 0.18)
    return jnp.clip(raised(array, jax.random.fold_in(stream_key, 3), *heavy), -limit, limit).astype(kind)


def setup_inputs(seed: int = 0) -> dict:
    streams_of = jax.random.split(jax.random.key(seed), 6)
    return {
        "query_input": draw_query_input(jax.random.fold_in(streams_of[5], 71), 0),
        "key_input": draw_key_input(jax.random.fold_in(streams_of[5], 71), 0),
        "value_input": draw_value_input(jax.random.fold_in(streams_of[5], 71), 0),
        "out_weight": noise_with(streams_of[3], (D, D), D ** -0.5, 0.125, ((0, 8),), (0, 1, 8, 2.0)),
        "out_cotangent": noise_with(streams_of[4], (SEQ, D), 1.0, 6.0, ((0, 32), (1, 8)), (0, 1, 32, 2.75)),
    }


LOG_TWO = math.log(2.0)


def rounded(tensor):
    return lax.optimization_barrier(tensor.astype(jnp.bfloat16)).astype(jnp.float32)


def coarse(tensor, factor):
    if factor == 1:
        return tensor
    row_count = tensor.shape[0] // factor
    blocked = tensor.reshape(row_count, factor, tensor.shape[1], tensor.shape[2]).astype(jnp.float32)
    return (jnp.sum(blocked, axis=1) * (1.0 / factor)).astype(jnp.bfloat16)


def own_blocks(tensor):
    return tensor.reshape(tensor.shape[0] // BLK, BLK, tensor.shape[1], tensor.shape[2])


def partner_blocks(tensor):
    block_count = tensor.shape[0] // BLK
    paired = tensor.reshape(block_count // 2, 2, BLK, tensor.shape[1], tensor.shape[2])
    return jnp.flip(paired, 1).reshape(block_count, BLK, tensor.shape[1], tensor.shape[2])


def unpair(grouped):
    block_count = grouped.shape[0]
    paired = grouped.reshape(block_count // 2, 2, BLK, grouped.shape[2], grouped.shape[3])
    return jnp.flip(paired, 1).reshape(block_count * BLK, grouped.shape[2], grouped.shape[3])


def level_groups(coarse_q, coarse_k, coarse_v, level_index):
    queries = own_blocks(coarse_q)
    key_rows = partner_blocks(coarse_k)
    value_rows = partner_blocks(coarse_v)
    if level_index == 0:
        key_rows = jnp.concatenate([own_blocks(coarse_k), key_rows], 1)
        value_rows = jnp.concatenate([own_blocks(coarse_v), value_rows], 1)
    return queries, key_rows, value_rows


def score_block(queries, key_rows, log_shift):
    scores = jnp.einsum("gqhd,gkhd->gqhk", queries.astype(jnp.float32), key_rows.astype(jnp.float32))
    return scores * (DH ** -0.5) + log_shift


def level_forward(queries, key_rows, value_rows, log_shift):
    scores = score_block(queries, key_rows, log_shift)
    row_peak = jnp.max(scores, axis=-1)
    exponent = jnp.exp(scores - row_peak[..., None])
    row_total = jnp.sum(exponent, axis=-1)
    weighted = jnp.einsum("gqhk,gkhd->gqhd", rounded(exponent), value_rows.astype(jnp.float32))
    return row_peak, row_total, weighted


def level_backward(queries, key_rows, value_rows, log_shift, row_peak, row_grad, row_scalar):
    score_scale = DH ** -0.5
    exponent = jnp.exp(score_block(queries, key_rows, log_shift) - row_peak[..., None])
    grad_float = row_grad.astype(jnp.float32)
    grad_weights = jnp.einsum("gqhd,gkhd->gqhk", grad_float, value_rows.astype(jnp.float32))
    grad_scores = rounded(exponent * (grad_weights - row_scalar[..., None]))
    query_part = jnp.einsum("gqhk,gkhd->gqhd", grad_scores, key_rows.astype(jnp.float32)) * score_scale
    key_part = jnp.einsum("gqhk,gqhd->gkhd", grad_scores, queries.astype(jnp.float32)) * score_scale
    value_part = jnp.einsum("gqhk,gqhd->gkhd", rounded(exponent), grad_float)
    return query_part, key_part, value_part


def forward_slab(query_slab, key_slab, value_slab):
    records = []
    for level_index in range(LEVELS):
        factor = 2 ** level_index
        groups = level_groups(coarse(query_slab, factor), coarse(key_slab, factor), coarse(value_slab, factor), level_index)
        row_peak, row_total, weighted = level_forward(groups[0], groups[1], groups[2], level_index * LOG_TWO)
        records.append((row_peak, row_total, weighted, groups))
    return records


def combine(records, token_count):
    expanded = []
    for level_index, record in enumerate(records):
        factor = 2 ** level_index
        expanded.append(jnp.repeat(record[0].reshape(token_count // factor, -1), factor, axis=0))
    highest = expanded[0]
    for expanded_peak in expanded[1:]:
        highest = jnp.maximum(highest, expanded_peak)
    scales = [jnp.exp(expanded_peak - highest) for expanded_peak in expanded]
    denominator = jnp.zeros_like(highest)
    numerator = jnp.zeros((token_count, records[0][2].shape[2], records[0][2].shape[3]), highest.dtype)
    for level_index, record in enumerate(records):
        factor = 2 ** level_index
        row_count = token_count // factor
        row_total = jnp.repeat(record[1].reshape(row_count, -1), factor, axis=0)
        weighted = jnp.repeat(record[2].reshape(row_count, record[2].shape[2], record[2].shape[3]), factor, axis=0)
        denominator = denominator + scales[level_index] * row_total
        numerator = numerator + scales[level_index][..., None] * weighted
    return numerator / denominator[..., None], scales, denominator


def backward_slab(query_slab, key_slab, value_slab, grad_slab):
    records = forward_slab(query_slab, key_slab, value_slab)
    token_count = query_slab.shape[0]
    heads_count = query_slab.shape[1]
    attn_f, scales, denominator = combine(records, token_count)
    grad_f = grad_slab.astype(jnp.float32)
    row_delta = jnp.sum(grad_f * attn_f, axis=-1)
    grad_q = jnp.zeros_like(attn_f)
    grad_k = jnp.zeros_like(attn_f)
    grad_v = jnp.zeros_like(attn_f)
    for level_index, record in enumerate(records):
        factor = 2 ** level_index
        row_count = token_count // factor
        level_share = scales[level_index] / denominator
        row_grad = jnp.sum((level_share[..., None] * grad_f).reshape(row_count, factor, heads_count, DH), axis=1).astype(jnp.bfloat16)
        row_scalar = jnp.sum((level_share * row_delta).reshape(row_count, factor, heads_count), axis=1)
        queries, key_rows, value_rows = record[3]
        block_count = queries.shape[0]
        query_part, key_part, value_part = level_backward(queries, key_rows, value_rows, level_index * LOG_TWO, record[0], row_grad.reshape(block_count, -1, heads_count, DH), row_scalar.reshape(block_count, -1, heads_count))
        query_coarse = query_part.reshape(row_count, heads_count, DH)
        if level_index == 0:
            key_coarse = key_part[:, :BLK].reshape(row_count, heads_count, DH) + unpair(key_part[:, BLK:])
            value_coarse = value_part[:, :BLK].reshape(row_count, heads_count, DH) + unpair(value_part[:, BLK:])
        else:
            key_coarse = unpair(key_part)
            value_coarse = unpair(value_part)
        inverse = 1.0 / factor
        grad_q = grad_q + jnp.repeat(query_coarse, factor, axis=0) * inverse
        grad_k = grad_k + jnp.repeat(key_coarse, factor, axis=0) * inverse
        grad_v = grad_v + jnp.repeat(value_coarse, factor, axis=0) * inverse
    return grad_q, grad_k, grad_v


def by_head(tensor):
    return jnp.transpose(tensor.reshape(SEQ, H, DH), (1, 0, 2))[:, :, None, :]


def from_head(tensor):
    return jnp.transpose(tensor[:, :, 0, :], (1, 0, 2)).reshape(SEQ, D)


def forward_head(slabs):
    records = forward_slab(slabs[0], slabs[1], slabs[2])
    attn_f = combine(records, SEQ)[0]
    peaks = jnp.stack([jnp.max(record[0]) - level_index * LOG_TWO for level_index, record in enumerate(records)])
    return attn_f, peaks


def backward_head(slabs):
    return backward_slab(slabs[0], slabs[1], slabs[2], slabs[3])


def reference(query_input, key_input, value_input, out_weight, out_cotangent):
    query_heads = by_head(query_input)
    key_heads = by_head(key_input)
    value_heads = by_head(value_input)
    attn_heads, peaks = lax.map(forward_head, (query_heads, key_heads, value_heads))
    attn = from_head(attn_heads).astype(jnp.bfloat16)
    mixed = jnp.dot(attn, out_weight, preferred_element_type=jnp.float32)
    grad_attn = jnp.dot(out_cotangent, out_weight.T, preferred_element_type=jnp.float32).astype(jnp.bfloat16)
    weight_grad = jnp.dot(attn.T, out_cotangent, preferred_element_type=jnp.float32)
    grads = lax.map(backward_head, (query_heads, key_heads, value_heads, by_head(grad_attn)))
    grad_q = from_head(grads[0])
    grad_k = from_head(grads[1])
    grad_v = from_head(grads[2])
    level_max = jnp.transpose(peaks)
    return mixed, grad_q, grad_k, grad_v, weight_grad, level_max
```

```python
import functools
import math

import jax
import jax.numpy as jnp
from jax import lax
from jax.experimental import pallas as pl
from jax.experimental.pallas import tpu as pltpu
from jax.sharding import PartitionSpec as P

DH = 128
BLK = 128
LEVELS = 5
NZ = 8
NCTX = 32
CHIPS = 16
HEADS = 4
TOK = 512
WID = HEADS * DH
HALF = TOK // 2
LOG_TWO = math.log(2.0)
SCALE = DH ** (-0.5)
MESH = pl.DeviceIdType.MESH
BF = jnp.bfloat16
F32 = jnp.float32
OFF = (0, 512, 768, 896, 960)
ROWS = 992


def dot(a, b):
    return lax.dot_general(a, b, (((1,), (0,)), ((), ())), preferred_element_type=F32)


def dot_nt(a, b):
    return lax.dot_general(a, b, (((1,), (1,)), ((), ())), preferred_element_type=F32)


def dot_tn(a, b):
    return lax.dot_general(a, b, (((0,), (0,)), ((), ())), preferred_element_type=F32)


def rows_of(start, size):
    return pl.ds(pl.multiple_of(start, size), size)


def expand(x, slabs):
    n = x.shape[0]
    if n == slabs:
        return x
    return jnp.broadcast_to(x[:, None], (n, slabs // n, 8, x.shape[2])).reshape(
        slabs, 8, x.shape[2]
    )


def halve(x):
    y = x.reshape(x.shape[0] // 2, 2, 8, x.shape[2])
    return y[:, 0] + y[:, 1]


def kernel(
    q_in, k_in, v_in, w_in, c_in,
    mixed, gq_out, gk_out, gv_out, wg_out, lm_out,
    qkv, perm, unperm, qkvp, pool1, qc2, qc3, p4, qc4, kvs2, kvs3, kvs4, kvr,
    e0, e1, e2, e3, e4, pk, tt, nm, wts5, af, ap, attn, attnt,
    cotg, wb, gacc, gp, wtile, wown, sibs, sibr, wsend, wrecv, wmine,
    rss, rsr, gqp, gkp, gvp, gks, gkr2, gkr3, gkr4, lmt, lmsib, lm2, lmr,
    in_sem, w_sem, c_sem, ag_s, ag_r, kv_s, kv_r, gk_s, gk_r,
    sib_s, sib_r, w_s, w_r, rs_s, rs_r, lmsib_s, lmsib_r, lm_s, lm_r,
):
    c = lax.axis_index("ctx")
    z = lax.axis_index("head")
    core = c % 2
    chip = c // 2

    def flipped(m):
        out = c
        for bit in range(3):
            if m >> bit & 1:
                out = out + (1 - 2 * (c // 2**bit % 2)) * 2**bit
        return out

    c_copy = pltpu.make_async_copy(c_in, cotg.at[z], c_sem)
    c_copy.start()
    in_copies = [
        pltpu.make_async_copy(src, qkv.at[t], in_sem.at[t])
        for t, src in enumerate((q_in, k_in, v_in))
    ]
    for copy in in_copies:
        copy.start()
    w_copies = [
        pltpu.make_async_copy(w_in.at[:, pl.ds(j * WID, WID)], wb.at[j], w_sem.at[j])
        for j in range(NZ)
    ]
    for copy in w_copies:
        copy.start()

    barrier = pltpu.get_barrier_semaphore()
    for step in (1, NZ - 1):
        pl.semaphore_signal(
            barrier, inc=1, device_id={"head": (z + step) % NZ}, device_id_type=MESH
        )
    for m in range(1, 8):
        pl.semaphore_signal(barrier, inc=1, device_id={"ctx": flipped(m)}, device_id_type=MESH)

    def greet(j, carry):
        pl.semaphore_signal(
            barrier,
            inc=1,
            device_id={"ctx": (chip + j) % CHIPS * 2 + core},
            device_id_type=MESH,
        )
        return carry

    lax.fori_loop(1, CHIPS, greet, 0)
    pl.semaphore_wait(barrier, 2 + 7 + CHIPS - 1)

    def ag_region(d, block, chunk):
        return cotg.at[block, rows_of(chunk * HALF, HALF), :]

    def ag_chunk(d, i):
        return i % 2 if d == 0 else 1 - i % 2

    def ag_send(d, i):
        if d == 0:
            block, to = (z + NZ - i // 2) % NZ, (z + 1) % NZ
        else:
            block, to = (z + i // 2) % NZ, (z + NZ - 1) % NZ
        region = ag_region(d, block, ag_chunk(d, i))
        return pltpu.make_async_remote_copy(
            src_ref=region, dst_ref=region, send_sem=ag_s.at[d, i], recv_sem=ag_r.at[d, i],
            device_id={"head": to}, device_id_type=MESH,
        )

    def ag_arrive(d, i):
        if d == 0:
            block = (z + 2 * NZ - 1 - i // 2) % NZ
        else:
            block = (z + 1 + i // 2) % NZ
        region = ag_region(d, block, ag_chunk(d, i))
        pltpu.make_async_remote_copy(
            src_ref=region, dst_ref=region, send_sem=ag_s.at[d, i], recv_sem=ag_r.at[d, i],
            device_id={"head": (z + 1) % NZ}, device_id_type=MESH,
        ).wait_recv()

    def ag_forward(i):
        for d in range(2):
            ag_arrive(d, i)
            ag_send(d, i + 2).start()

    c_copy.wait()
    for i in range(2):
        for d in range(2):
            ag_send(d, i).start()

    row_id = lax.broadcasted_iota(jnp.int32, (BLK, BLK), 0)
    col_id = lax.broadcasted_iota(jnp.int32, (BLK, BLK), 1)
    perm[...] = jnp.where(col_id == row_id % 8 * 16 + row_id // 8, 1.0, 0.0).astype(BF)
    unperm[...] = jnp.where(row_id == col_id % 8 * 16 + col_id // 8, 1.0, 0.0).astype(BF)
    lmt[...] = jnp.full((8, DH), -3.0e38, F32)

    for t in (1, 2, 0):
        in_copies[t].wait()

        def pool(b, carry, t=t):
            x = dot(perm[...], qkv[t, rows_of(b * BLK, BLK), :])
            qkvp[t, rows_of(b * BLK, BLK), :] = x.astype(BF)
            one = halve(x.reshape(16, 8, WID))
            pool1[t, rows_of(b * 64, 64), :] = (one * 0.5).reshape(64, WID).astype(BF)
            two = halve(one)
            two_rows = (two * 0.25).reshape(32, WID).astype(BF)
            three = halve(two)
            three_rows = (three * 0.125).reshape(16, WID).astype(BF)
            if t == 0:
                qc2[rows_of(b * 32, 32), :] = two_rows
                qc3[rows_of(b * 16, 16), :] = three_rows
            else:
                kvs2[t - 1, rows_of(b * 32, 32), :] = two_rows
                kvs3[t - 1, rows_of(b * 16, 16), :] = three_rows
            p4[t, rows_of(b * 8, 8), :] = (halve(three) * 0.0625).reshape(8, WID)
            return carry

        lax.fori_loop(0, 4, pool, 0)
        if t == 0:
            qc4[...] = p4[0].astype(BF)
        else:
            kvs4[t - 1] = p4[t].astype(BF)

        if t == 2:
            kv_sends = []
            for m in range(1, 8):
                if m == 1:
                    src, dst, slot = kvs2, kvr.at[0], 0
                elif m < 4:
                    src, slot = kvs3, 1 + core
                    dst = kvr.at[1, :, rows_of(core * 64, 64), :]
                else:
                    src, slot = kvs4, 3 + c % 4
                    dst = kvr.at[2, :, rows_of(c % 4 * 32, 32), :]
                copy = pltpu.make_async_remote_copy(
                    src_ref=src, dst_ref=dst, send_sem=kv_s.at[m], recv_sem=kv_r.at[slot],
                    device_id={"ctx": flipped(m)}, device_id_type=MESH,
                )
                copy.start()
                kv_sends.append(copy)

    def kv_arrive():
        for slot in range(7):
            if slot == 0:
                src, dst = kvs2, kvr.at[0]
            elif slot < 3:
                src, dst = kvs3, kvr.at[1, :, pl.ds((slot - 1) * 64, 64), :]
            else:
                src, dst = kvs4, kvr.at[2, :, pl.ds((slot - 3) * 32, 32), :]
            pltpu.make_async_remote_copy(
                src_ref=src, dst_ref=dst, send_sem=kv_s.at[1], recv_sem=kv_r.at[slot],
                device_id={"ctx": flipped(1)}, device_id_type=MESH,
            ).wait_recv()

    tile_row = lax.broadcasted_iota(jnp.int32, (8, DH), 0)
    tile_col = lax.broadcasted_iota(jnp.int32, (8, DH), 1)

    def attend(h, level, start, count, queries, keys, values):
        scores = dot_nt(queries, keys) * SCALE
        peak = jnp.max(scores, axis=-1, keepdims=True)
        e = jnp.exp(scores - peak)
        total = jnp.sum(e, axis=-1, keepdims=True)
        wide = jnp.broadcast_to(peak, (count, DH))
        at = pl.ds(start, count) if isinstance(start, int) else start
        pk[h, at, :] = wide + level * LOG_TWO
        tt[h, at, :] = jnp.broadcast_to(total, (count, DH))
        nm[h, at, :] = dot(e.astype(BF), values)
        top = jnp.max(wide.reshape(count // 8, 8, DH), axis=0)
        top = jnp.broadcast_to(jnp.max(top, axis=0, keepdims=True), (8, DH))
        here = jnp.logical_and(tile_row == level, tile_col == h)
        lmt[...] = jnp.where(here, jnp.maximum(lmt[...], top), lmt[...])
        return e

    def lanes(h):
        return rows_of(h * DH, DH)

    def near_forward(h, carry):
        hs = lanes(h)
        for p in range(2):
            at = pl.ds(p * 256, 256)
            e0[h, p] = attend(h, 0, p * 256, 256, qkvp[0, at, hs], qkvp[1, at, hs], qkvp[2, at, hs])
        for g in range(2):
            other = pl.ds((1 - g) * 128, 128)
            e1[h, g] = attend(
                h, 1, OFF[1] + g * 128, 128,
                pool1[0, pl.ds(g * 128, 128), hs], pool1[1, other, hs], pool1[2, other, hs],
            )
        return carry

    lax.fori_loop(0, HEADS, near_forward, 0)
    ag_forward(0)
    kv_arrive()

    def far_forward(h, carry):
        hs = lanes(h)
        for level, queries, store in ((2, qc2, e2), (3, qc3, e3), (4, qc4, e4)):
            count = TOK >> level
            store[h] = attend(
                h, level, OFF[level], count,
                queries[:, hs], kvr[level - 2, 0, :, hs], kvr[level - 2, 1, :, hs],
            )

        def merge(b, inner):
            def level_rows(ref, level):
                n = BLK >> level
                return expand(ref[h, rows_of(OFF[level] + b * n, n), :].reshape(n // 8, 8, DH), 16)

            peaks = [level_rows(pk, level) for level in range(LEVELS)]
            highest = peaks[0]
            for other in peaks[1:]:
                highest = jnp.maximum(highest, other)
            scales = [jnp.exp(peak - highest) for peak in peaks]
            den = scales[0] * level_rows(tt, 0)
            num = scales[0] * level_rows(nm, 0)
            for level in range(1, LEVELS):
                den = den + scales[level] * level_rows(tt, level)
                num = num + scales[level] * level_rows(nm, level)
            inv = 1.0 / den
            at = rows_of(b * BLK, BLK)
            for level in range(LEVELS):
                wts5[h, level, at, :] = (scales[level] * inv).reshape(BLK, DH)
            out = (num * inv).reshape(BLK, DH)
            af[h, at, :] = out
            ap[at, hs] = out.astype(BF)
            return inner

        lax.fori_loop(0, 4, merge, 0)
        return carry

    lax.fori_loop(0, HEADS, far_forward, 0)
    ag_forward(1)

    lmsib_copy = pltpu.make_async_remote_copy(
        src_ref=lmt, dst_ref=lmsib, send_sem=lmsib_s, recv_sem=lmsib_r,
        device_id={"ctx": flipped(1)}, device_id_type=MESH,
    )
    lmsib_copy.start()

    def restore(b, carry):
        at = rows_of(b * BLK, BLK)
        attn[at, :] = dot(unperm[...], ap[at, :]).astype(BF)
        return carry

    lax.fori_loop(0, 4, restore, 0)

    def turn(f, carry):
        attnt[rows_of(f * DH, DH), :] = attn[:, rows_of(f * DH, DH)].astype(F32).T.astype(BF)
        return carry

    lax.fori_loop(0, HEADS, turn, 0)
    for copy in w_copies:
        copy.wait()
    ag_forward(2)

    def sib_copy(block):
        return pltpu.make_async_remote_copy(
            src_ref=sibs.at[block], dst_ref=sibr.at[block],
            send_sem=sib_s.at[block], recv_sem=sib_r.at[block],
            device_id={"ctx": flipped(1)}, device_id_type=MESH,
        )

    def w_copy(to_chip, slot):
        return pltpu.make_async_remote_copy(
            src_ref=wsend.at[to_chip], dst_ref=wrecv.at[slot],
            send_sem=w_s.at[to_chip], recv_sem=w_r.at[slot],
            device_id={"ctx": to_chip * 2 + core}, device_id_type=MESH,
        )

    def block_terms(block, slot, first=False):
        def part(r, carry):
            at = rows_of(r * HALF, HALF)
            term = dot_nt(cotg[block, at, :], wb[block])
            gacc[at, :] = term if first else gacc[at, :] + term
            weight = dot(attnt[at, :], cotg[block])
            for m in range(4):
                wtile[m] = weight[:, m * DH : (m + 1) * DH]
            for i in range(2):
                wown[slot, i, at, :] = wtile[2 * i + core]
                sibs[block, i, at, :] = wtile[2 * i + 1 - core].astype(BF)
            return carry

        lax.fori_loop(0, 2, part, 0)
        sib_copy(block).start()

    def block_share(block, slot):
        sib_copy(block).wait_recv()
        for i in range(2):
            owner = 2 * block + i
            total = wown[slot, i] + sibr[block, i].astype(F32)

            @pl.when(owner == chip)
            def _():
                wmine[...] = total

            @pl.when(owner != chip)
            def _():
                wsend[owner] = total.astype(BF)
                w_copy(owner, chip).start()

    block_terms(z, 0, first=True)
    ag_forward(3)
    block_share(z, 0)

    def both(distance):
        def side(s, carry):
            block = (z + NZ + (1 - 2 * s) * distance) % NZ
            block_terms(block, s)
            block_share(block, s)
            return carry

        lax.fori_loop(0, 2, side, 0)

    both(1)
    ag_forward(4)

    def mixed_part(block, chunk):
        return dot(attn[rows_of(chunk * HALF, HALF), :], wb[block])

    def rs_copy(d, i):
        return pltpu.make_async_remote_copy(
            src_ref=rss.at[d, i], dst_ref=rsr.at[d, i],
            send_sem=rs_s.at[d, i], recv_sem=rs_r.at[d, i],
            device_id={"head": (z + 1) % NZ if d == 0 else (z + NZ - 1) % NZ},
            device_id_type=MESH,
        )

    def rs_send(d, i, relay):
        distance = 4 - (i + 1) // 2
        block = (z + distance) % NZ if d == 0 else (z + NZ - distance) % NZ
        value = mixed_part(block, ag_chunk(d, i))
        if relay:
            rs_copy(d, i - 2).wait_recv()
            value = value + rsr[d, i - 2].astype(F32)
        rss[d, i] = value.astype(BF)
        rs_copy(d, i).start()

    def rs_relay(i):
        for d in range(2):
            rs_send(d, i + 2, True)

    for i in range(2):
        for d in range(2):
            rs_send(d, i, False)

    lmsib_copy.wait()
    lm2[...] = jnp.maximum(lmt[...], lmsib[...])

    def lm_copy(to_chip, slot):
        return pltpu.make_async_remote_copy(
            src_ref=lm2, dst_ref=lmr.at[slot], send_sem=lm_s.at[to_chip], recv_sem=lm_r.at[slot],
            device_id={"ctx": to_chip * 2 + core}, device_id_type=MESH,
        )

    def lm_start(j, carry):
        lm_copy((chip + j) % CHIPS, chip).start()
        return carry

    lax.fori_loop(1, CHIPS, lm_start, 0)

    both(2)
    for d in range(2):
        ag_arrive(d, 5)
    both(3)
    for d in range(2):
        ag_arrive(d, 6)
    block_terms((z + 4) % NZ, 0)
    block_share((z + 4) % NZ, 0)

    def permute_grad(b, carry):
        at = rows_of(b * BLK, BLK)
        gp[at, :] = dot(perm[...], gacc[at, :].astype(BF)).astype(BF)
        return carry

    lax.fori_loop(0, 4, permute_grad, 0)

    rsc, dq, rg = pk, tt, nm

    def score_grads(h, level, at, e, queries, keys, values):
        grad = rg[h, at, :].astype(BF)
        weights = dot_nt(grad, values)
        dz = (e * (weights - rsc[h, at, :][:, :1])).astype(BF)
        dq[h, at, :] = dot(dz, keys) * (SCALE * 0.5**level)
        return dot_tn(dz, queries) * SCALE, dot_tn(e.astype(BF), grad)

    def far_backward(h, carry):
        hs = lanes(h)

        def spread(b, inner):
            at = rows_of(b * BLK, BLK)
            g = gp[at, hs].astype(F32)
            delta = jnp.sum(g * af[h, at, :], axis=-1, keepdims=True)
            g = g.reshape(16, 8, DH)
            delta = jnp.broadcast_to(delta, (BLK, DH)).reshape(16, 8, DH)
            for level in range(LEVELS):
                share = wts5[h, level, at, :].reshape(16, 8, DH)
                grads, scalars = share * g, share * delta
                for _ in range(level):
                    grads, scalars = halve(grads), halve(scalars)
                n = BLK >> level
                put = rows_of(OFF[level] + b * n, n)
                rg[h, put, :] = grads.reshape(n, DH)
                rsc[h, put, :] = scalars.reshape(n, DH)
            return inner

        lax.fori_loop(0, 4, spread, 0)
        for level, queries, store in ((2, qc2, e2), (3, qc3, e3), (4, qc4, e4)):
            dk, dv = score_grads(
                h, level, pl.ds(OFF[level], TOK >> level), store[h],
                queries[:, hs], kvr[level - 2, 0, :, hs], kvr[level - 2, 1, :, hs],
            )
            gks[level - 2, 0, :, hs] = (dk * 0.5**level).astype(BF)
            gks[level - 2, 1, :, hs] = (dv * 0.5**level).astype(BF)
        return carry

    lax.fori_loop(0, HEADS, far_backward, 0)

    gk_sends = []
    for m in range(1, 8):
        if m == 1:
            src, dst, slot = gks.at[0], gkr2, 0
        elif m < 4:
            src = gks.at[1, :, rows_of(flipped(m) % 2 * 64, 64), :]
            dst, slot = gkr3.at[core], 1 + core
        else:
            src = gks.at[2, :, rows_of(flipped(m) % 4 * 32, 32), :]
            dst, slot = gkr4.at[c % 4], 3 + c % 4
        copy = pltpu.make_async_remote_copy(
            src_ref=src, dst_ref=dst, send_sem=gk_s.at[m], recv_sem=gk_r.at[slot],
            device_id={"ctx": flipped(m)}, device_id_type=MESH,
        )
        copy.start()
        gk_sends.append(copy)

    rs_relay(0)

    def near_backward(h, carry):
        hs = lanes(h)
        for p in range(2):
            at = pl.ds(p * 256, 256)
            dk, dv = score_grads(
                h, 0, at, e0[h, p], qkvp[0, at, hs], qkvp[1, at, hs], qkvp[2, at, hs]
            )
            gkp[at, hs] = dk
            gvp[at, hs] = dv
        for g in range(2):
            other = pl.ds((1 - g) * 128, 128)
            dk, dv = score_grads(
                h, 1, pl.ds(OFF[1] + g * 128, 128), e1[h, g],
                pool1[0, pl.ds(g * 128, 128), hs], pool1[1, other, hs], pool1[2, other, hs],
            )
            to = pl.ds((1 - g) * 256, 256)
            for ref, part in ((gkp, dk), (gvp, dv)):
                wide = expand((part * 0.5).reshape(16, 8, DH), 32).reshape(256, DH)
                ref[to, hs] = ref[to, hs] + wide

        def gather_q(b, inner):
            total = dq[h, rows_of(b * BLK, BLK), :].reshape(16, 8, DH)
            for level in range(1, LEVELS):
                n = BLK >> level
                part = dq[h, rows_of(OFF[level] + b * n, n), :].reshape(n // 8, 8, DH)
                total = total + expand(part, 16)
            gqp[rows_of(b * BLK, BLK), hs] = total.reshape(BLK, DH)
            return inner

        lax.fori_loop(0, 4, gather_q, 0)
        return carry

    lax.fori_loop(0, HEADS, near_backward, 0)
    rs_relay(1)

    def token_order(x):
        high = x.astype(BF)
        low = (x - high.astype(F32)).astype(BF)
        return dot(unperm[...], high) + dot(unperm[...], low)

    def finish_q(b, carry):
        at = rows_of(b * BLK, BLK)
        gq_out[at, :] = token_order(gqp[at, :])
        return carry

    lax.fori_loop(0, 4, finish_q, 0)
    rs_relay(2)

    for slot in range(7):
        if slot == 0:
            src, dst = gks.at[0], gkr2
        elif slot < 3:
            src, dst = gks.at[1, :, pl.ds(0, 64), :], gkr3.at[slot - 1]
        else:
            src, dst = gks.at[2, :, pl.ds(0, 32), :], gkr4.at[slot - 3]
        pltpu.make_async_remote_copy(
            src_ref=src, dst_ref=dst, send_sem=gk_s.at[1], recv_sem=gk_r.at[slot],
            device_id={"ctx": flipped(1)}, device_id_type=MESH,
        ).wait_recv()

    for t, (own, out) in enumerate(((gkp, gk_out), (gvp, gv_out))):
        p4[t] = sum(gkr4[s, t].astype(F32) for s in range(4))

        def finish_kv(b, carry, t=t, own=own, out=out):
            at = rows_of(b * BLK, BLK)
            two = gkr2[t, rows_of(b * 32, 32), :].astype(F32)
            three = gkr3[0, t, rows_of(b * 16, 16), :].astype(F32)
            three = three + gkr3[1, t, rows_of(b * 16, 16), :].astype(F32)
            four = p4[t, rows_of(b * 8, 8), :]
            low = expand(three.reshape(2, 8, WID), 4) + expand(four.reshape(1, 8, WID), 4)
            low = low + two.reshape(4, 8, WID)
            total = own[at, :] + expand(low, 16).reshape(BLK, WID)
            out[at, :] = token_order(total)
            return carry

        lax.fori_loop(0, 4, finish_kv, 0)

    rs_relay(3)

    def w_sum(j, carry):
        slot = (chip + j) % CHIPS
        w_copy(chip, slot).wait_recv()
        wmine[...] = wmine[...] + wrecv[slot].astype(F32)
        return carry

    lax.fori_loop(1, CHIPS, w_sum, 0)
    wg_out[...] = wmine[...]

    def lm_max(j, carry):
        slot = (chip + j) % CHIPS
        lm_copy(chip, slot).wait_recv()
        lmt[...] = jnp.maximum(lmt[...], lmr[slot])
        return carry

    lmt[...] = lm2[...]
    lax.fori_loop(1, CHIPS, lm_max, 0)
    lm_out[...] = lmt[...][:LEVELS, :HEADS]

    rs_relay(4)
    low = mixed_part(z, 0)
    high = mixed_part(z, 1)
    mixed[pl.ds(0, HALF), :] = low
    mixed[pl.ds(HALF, HALF), :] = high
    for i, chunks in ((5, (1, 0)), (6, (0, 1))):
        for d in range(2):
            rs_copy(d, i).wait_recv()
            at = pl.ds(chunks[d] * HALF, HALF)
            mixed[at, :] = mixed[at, :] + rsr[d, i].astype(F32)

    for copy in kv_sends + gk_sends:
        copy.wait_send()

    def drain(i, carry):
        for d in range(2):
            ag_send(d, i).wait_send()
            rs_copy(d, i).wait_send()
        return carry

    lax.fori_loop(0, 7, drain, 0)

    def drain_sib(i, carry):
        sib_copy(i).wait_send()
        return carry

    lax.fori_loop(0, NZ, drain_sib, 0)

    def drain_chips(j, carry):
        to = (chip + j) % CHIPS
        w_copy(to, chip).wait_send()
        lm_copy(to, chip).wait_send()
        return carry

    lax.fori_loop(1, CHIPS, drain_chips, 0)


def vmem(shape, kind):
    return pltpu.VMEM(shape, kind)


def per_device(query_input, key_input, value_input, out_weight, out_cotangent):
    dma = pltpu.SemaphoreType.DMA
    scratch = [
        vmem((3, TOK, WID), BF),
        vmem((BLK, BLK), BF),
        vmem((BLK, BLK), BF),
        vmem((3, TOK, WID), BF),
        vmem((3, 256, WID), BF),
        vmem((128, WID), BF),
        vmem((64, WID), BF),
        vmem((3, 32, WID), F32),
        vmem((32, WID), BF),
        vmem((2, 128, WID), BF),
        vmem((2, 64, WID), BF),
        vmem((2, 32, WID), BF),
        vmem((3, 2, 128, WID), BF),
        vmem((HEADS, 2, 256, 256), F32),
        vmem((HEADS, 2, 128, 128), F32),
        vmem((HEADS, 128, 128), F32),
        vmem((HEADS, 64, 128), F32),
        vmem((HEADS, 32, 128), F32),
        vmem((HEADS, ROWS, DH), F32),
        vmem((HEADS, ROWS, DH), F32),
        vmem((HEADS, ROWS, DH), F32),
        vmem((HEADS, LEVELS, TOK, DH), F32),
        vmem((HEADS, TOK, DH), F32),
        vmem((TOK, WID), BF),
        vmem((TOK, WID), BF),
        vmem((WID, TOK), BF),
        vmem((NZ, TOK, WID), BF),
        vmem((NZ, WID, WID), BF),
        vmem((TOK, WID), F32),
        vmem((TOK, WID), BF),
        vmem((4, HALF, DH), F32),
        vmem((2, 2, WID, DH), F32),
        vmem((NZ, 2, WID, DH), BF),
        vmem((NZ, 2, WID, DH), BF),
        vmem((CHIPS, WID, DH), BF),
        vmem((CHIPS, WID, DH), BF),
        vmem((WID, DH), F32),
        vmem((2, 7, HALF, WID), BF),
        vmem((2, 7, HALF, WID), BF),
        vmem((TOK, WID), F32),
        vmem((TOK, WID), F32),
        vmem((TOK, WID), F32),
        vmem((3, 2, 128, WID), BF),
        vmem((2, 128, WID), BF),
        vmem((2, 2, 64, WID), BF),
        vmem((4, 2, 32, WID), BF),
        vmem((8, DH), F32),
        vmem((8, DH), F32),
        vmem((8, DH), F32),
        vmem((CHIPS, 8, DH), F32),
        dma((3,)), dma((NZ,)), dma,
        dma((2, 7)), dma((2, 7)),
        dma((8,)), dma((7,)), dma((8,)), dma((7,)),
        dma((NZ,)), dma((NZ,)), dma((CHIPS,)), dma((CHIPS,)),
        dma((2, 7)), dma((2, 7)),
        dma, dma, dma((CHIPS,)), dma((CHIPS,)),
    ]
    wide = jax.ShapeDtypeStruct((TOK, WID), F32)
    return pl.pallas_call(
        kernel,
        out_shape=(
            wide, wide, wide, wide,
            jax.ShapeDtypeStruct((WID, DH), F32),
            jax.ShapeDtypeStruct((LEVELS, HEADS), F32),
        ),
        in_specs=[pl.BlockSpec(memory_space=pl.ANY)] * 5,
        out_specs=[pl.BlockSpec(memory_space=pltpu.VMEM)] * 6,
        scratch_shapes=scratch,
        compiler_params=pltpu.CompilerParams(
            collective_id=0, has_side_effects=True, vmem_limit_bytes=67000000
        ),
        name="layer",
    )(query_input, key_input, value_input, out_weight, out_cotangent)


def solution(mesh):
    in_specs = (
        P("ctx", "head"),
        P("ctx", "head"),
        P("ctx", "head"),
        P("head", None),
        P("ctx", "head"),
    )
    out_specs = (
        P("ctx", "head"),
        P("ctx", "head"),
        P("ctx", "head"),
        P("ctx", "head"),
        P("head", "ctx"),
        P(None, "head"),
    )
    return jax.shard_map(
        per_device, mesh=mesh, in_specs=in_specs, out_specs=out_specs, check_vma=False
    )
```

```python
import functools
import math

import jax
import jax.numpy as jnp
from jax import lax
from jax.experimental import pallas as pl
from jax.experimental.pallas import tpu as pltpu
from jax.sharding import PartitionSpec as P

DH = 128
BLK = 128
LEVELS = 5
NZ = 8
NCTX = 32
CHIPS = 16
HEADS = 4
TOK = 512
WID = HEADS * DH
HALF = TOK // 2
LOG_TWO = math.log(2.0)
SCALE = DH ** (-0.5)
MESH = pl.DeviceIdType.MESH
BF = jnp.bfloat16
F32 = jnp.float32
OFF = (0, 512, 768, 896, 960)
ROWS = 992


def dot(a, b):
    return lax.dot_general(a, b, (((1,), (0,)), ((), ())), preferred_element_type=F32)


def dot_nt(a, b):
    return lax.dot_general(a, b, (((1,), (1,)), ((), ())), preferred_element_type=F32)


def dot_tn(a, b):
    return lax.dot_general(a, b, (((0,), (0,)), ((), ())), preferred_element_type=F32)


def rows_of(start, size):
    return pl.ds(pl.multiple_of(start, size), size)


def expand(x, slabs):
    n = x.shape[0]
    if n == slabs:
        return x
    return jnp.broadcast_to(x[:, None], (n, slabs // n, 8, x.shape[2])).reshape(
        slabs, 8, x.shape[2]
    )


def halve(x):
    y = x.reshape(x.shape[0] // 2, 2, 8, x.shape[2])
    return y[:, 0] + y[:, 1]


def kernel(
    q_in, k_in, v_in, w_in, c_in,
    mix, gqp, gkp, gvp, wmine, lm_out,
    qkv, perm, unperm, qkvp, pool1, qc2, qc3, p4, qc4, kvs2, kvs3, kvs4, kvr,
    e0, e1, e2, e3, e4, pk, tt, nm, wts5, af, ap, attn, attnt,
    cotg, wb, gacc, gp, wtile, wown, sibs, sibr, wsend, wrecv,
    rss, rsr, gks, gkr2, gkr3, gkr4, lmt, lmsib, lm2, lmr,
    in_sem, w_sem, c_sem, ag_s, ag_r, kv_s, kv_r, gk_s, gk_r,
    sib_s, sib_r, w_s, w_r, rs_s, rs_r, lmsib_s, lmsib_r, lm_s, lm_r,
):
    c = lax.axis_index("ctx")
    z = lax.axis_index("head")
    core = c % 2
    chip = c // 2

    def flipped(m):
        out = c
        for bit in range(3):
            if m >> bit & 1:
                out = out + (1 - 2 * (c // 2**bit % 2)) * 2**bit
        return out

    c_copy = pltpu.make_async_copy(c_in, cotg.at[z], c_sem)
    c_copy.start()
    in_copies = [
        pltpu.make_async_copy(src, qkv.at[t], in_sem.at[t])
        for t, src in enumerate((q_in, k_in, v_in))
    ]
    for copy in in_copies:
        copy.start()
    w_copies = [
        pltpu.make_async_copy(w_in.at[:, pl.ds(j * WID, WID)], wb.at[j], w_sem.at[j])
        for j in range(NZ)
    ]
    for copy in w_copies:
        copy.start()

    barrier = pltpu.get_barrier_semaphore()
    for step in (1, NZ - 1):
        pl.semaphore_signal(
            barrier, inc=1, device_id={"head": (z + step) % NZ}, device_id_type=MESH
        )
    for m in range(1, 8):
        pl.semaphore_signal(barrier, inc=1, device_id={"ctx": flipped(m)}, device_id_type=MESH)

    def greet(j, carry):
        pl.semaphore_signal(
            barrier,
            inc=1,
            device_id={"ctx": (chip + j) % CHIPS * 2 + core},
            device_id_type=MESH,
        )
        return carry

    lax.fori_loop(1, CHIPS, greet, 0)
    pl.semaphore_wait(barrier, 2 + 7 + CHIPS - 1)

    def ag_region(d, block, chunk):
        return cotg.at[block, rows_of(chunk * HALF, HALF), :]

    def ag_chunk(d, i):
        return i % 2 if d == 0 else 1 - i % 2

    def ag_send(d, i):
        if d == 0:
            block, to = (z + NZ - i // 2) % NZ, (z + 1) % NZ
        else:
            block, to = (z + i // 2) % NZ, (z + NZ - 1) % NZ
        region = ag_region(d, block, ag_chunk(d, i))
        return pltpu.make_async_remote_copy(
            src_ref=region, dst_ref=region, send_sem=ag_s.at[d, i], recv_sem=ag_r.at[d, i],
            device_id={"head": to}, device_id_type=MESH,
        )

    def ag_arrive(d, i):
        if d == 0:
            block = (z + 2 * NZ - 1 - i // 2) % NZ
        else:
            block = (z + 1 + i // 2) % NZ
        region = ag_region(d, block, ag_chunk(d, i))
        pltpu.make_async_remote_copy(
            src_ref=region, dst_ref=region, send_sem=ag_s.at[d, i], recv_sem=ag_r.at[d, i],
            device_id={"head": (z + 1) % NZ}, device_id_type=MESH,
        ).wait_recv()

    def ag_forward(i):
        for d in range(2):
            ag_arrive(d, i)
            ag_send(d, i + 2).start()

    c_copy.wait()
    for i in range(2):
        for d in range(2):
            ag_send(d, i).start()

    row_id = lax.broadcasted_iota(jnp.int32, (BLK, BLK), 0)
    col_id = lax.broadcasted_iota(jnp.int32, (BLK, BLK), 1)
    perm[...] = jnp.where(col_id == row_id % 8 * 16 + row_id // 8, 1.0, 0.0).astype(BF)
    unperm[...] = jnp.where(row_id == col_id % 8 * 16 + col_id // 8, 1.0, 0.0).astype(BF)
    lmt[...] = jnp.full((8, DH), -3.0e38, F32)

    for t in (1, 2, 0):
        in_copies[t].wait()

        def pool(b, carry, t=t):
            x = dot(perm[...], qkv[t, rows_of(b * BLK, BLK), :])
            qkvp[t, rows_of(b * BLK, BLK), :] = x.astype(BF)
            one = halve(x.reshape(16, 8, WID))
            pool1[t, rows_of(b * 64, 64), :] = (one * 0.5).reshape(64, WID).astype(BF)
            two = halve(one)
            two_rows = (two * 0.25).reshape(32, WID).astype(BF)
            three = halve(two)
            three_rows = (three * 0.125).reshape(16, WID).astype(BF)
            if t == 0:
                qc2[rows_of(b * 32, 32), :] = two_rows
                qc3[rows_of(b * 16, 16), :] = three_rows
            else:
                kvs2[t - 1, rows_of(b * 32, 32), :] = two_rows
                kvs3[t - 1, rows_of(b * 16, 16), :] = three_rows
            p4[t, rows_of(b * 8, 8), :] = (halve(three) * 0.0625).reshape(8, WID)
            return carry

        lax.fori_loop(0, 4, pool, 0)
        if t == 0:
            qc4[...] = p4[0].astype(BF)
        else:
            kvs4[t - 1] = p4[t].astype(BF)

        if t == 2:
            kv_sends = []
            for m in range(1, 8):
                if m == 1:
                    src, dst, slot = kvs2, kvr.at[0], 0
                elif m < 4:
                    src, slot = kvs3, 1 + core
                    dst = kvr.at[1, :, rows_of(core * 64, 64), :]
                else:
                    src, slot = kvs4, 3 + c % 4
                    dst = kvr.at[2, :, rows_of(c % 4 * 32, 32), :]
                copy = pltpu.make_async_remote_copy(
                    src_ref=src, dst_ref=dst, send_sem=kv_s.at[m], recv_sem=kv_r.at[slot],
                    device_id={"ctx": flipped(m)}, device_id_type=MESH,
                )
                copy.start()
                kv_sends.append(copy)

    def kv_arrive():
        for slot in range(7):
            if slot == 0:
                src, dst = kvs2, kvr.at[0]
            elif slot < 3:
                src, dst = kvs3, kvr.at[1, :, pl.ds((slot - 1) * 64, 64), :]
            else:
                src, dst = kvs4, kvr.at[2, :, pl.ds((slot - 3) * 32, 32), :]
            pltpu.make_async_remote_copy(
                src_ref=src, dst_ref=dst, send_sem=kv_s.at[1], recv_sem=kv_r.at[slot],
                device_id={"ctx": flipped(1)}, device_id_type=MESH,
            ).wait_recv()

    tile_row = lax.broadcasted_iota(jnp.int32, (8, DH), 0)
    tile_col = lax.broadcasted_iota(jnp.int32, (8, DH), 1)

    def attend(h, level, start, count, queries, keys, values):
        scores = dot_nt(queries, keys) * SCALE
        peak = jnp.max(scores, axis=-1, keepdims=True)
        e = jnp.exp(scores - peak)
        total = jnp.sum(e, axis=-1, keepdims=True)
        wide = jnp.broadcast_to(peak, (count, DH))
        at = pl.ds(start, count) if isinstance(start, int) else start
        pk[h, at, :] = wide + level * LOG_TWO
        tt[h, at, :] = jnp.broadcast_to(total, (count, DH))
        nm[h, at, :] = dot(e.astype(BF), values)
        top = jnp.max(wide.reshape(count // 8, 8, DH), axis=0)
        top = jnp.broadcast_to(jnp.max(top, axis=0, keepdims=True), (8, DH))
        here = jnp.logical_and(tile_row == h, tile_col == level)
        lmt[...] = jnp.where(here, jnp.maximum(lmt[...], top), lmt[...])
        return e

    def lanes(h):
        return rows_of(h * DH, DH)

    def near_forward(h, carry):
        hs = lanes(h)
        for p in range(2):
            at = pl.ds(p * 256, 256)
            e0[h, p] = attend(h, 0, p * 256, 256, qkvp[0, at, hs], qkvp[1, at, hs], qkvp[2, at, hs])
        for g in range(2):
            other = pl.ds((1 - g) * 128, 128)
            e1[h, g] = attend(
                h, 1, OFF[1] + g * 128, 128,
                pool1[0, pl.ds(g * 128, 128), hs], pool1[1, other, hs], pool1[2, other, hs],
            )
        return carry

    lax.fori_loop(0, HEADS, near_forward, 0)
    ag_forward(0)
    ag_forward(1)
    kv_arrive()

    def far_forward(h, carry):
        hs = lanes(h)
        for level, queries, store in ((2, qc2, e2), (3, qc3, e3), (4, qc4, e4)):
            count = TOK >> level
            store[h] = attend(
                h, level, OFF[level], count,
                queries[:, hs], kvr[level - 2, 0, :, hs], kvr[level - 2, 1, :, hs],
            )

        def merge(b, inner):
            def level_rows(ref, level):
                n = BLK >> level
                return expand(ref[h, rows_of(OFF[level] + b * n, n), :].reshape(n // 8, 8, DH), 16)

            peaks = [level_rows(pk, level) for level in range(LEVELS)]
            highest = peaks[0]
            for other in peaks[1:]:
                highest = jnp.maximum(highest, other)
            scales = [jnp.exp(peak - highest) for peak in peaks]
            den = scales[0] * level_rows(tt, 0)
            num = scales[0] * level_rows(nm, 0)
            for level in range(1, LEVELS):
                den = den + scales[level] * level_rows(tt, level)
                num = num + scales[level] * level_rows(nm, level)
            inv = 1.0 / den
            at = rows_of(b * BLK, BLK)
            for level in range(LEVELS):
                wts5[h, level, at, :] = (scales[level] * inv).reshape(BLK, DH)
            out = (num * inv).reshape(BLK, DH)
            af[h, at, :] = out
            ap[at, hs] = out.astype(BF)
            return inner

        lax.fori_loop(0, 4, merge, 0)
        return carry

    lax.fori_loop(0, HEADS, far_forward, 0)
    ag_forward(2)

    lmsib_copy = pltpu.make_async_remote_copy(
        src_ref=lmt, dst_ref=lmsib, send_sem=lmsib_s, recv_sem=lmsib_r,
        device_id={"ctx": flipped(1)}, device_id_type=MESH,
    )
    lmsib_copy.start()

    def restore(b, carry):
        at = rows_of(b * BLK, BLK)
        attn[at, :] = dot(unperm[...], ap[at, :]).astype(BF)
        return carry

    lax.fori_loop(0, 4, restore, 0)

    def turn(f, carry):
        attnt[rows_of(f * DH, DH), :] = attn[:, rows_of(f * DH, DH)].astype(F32).T.astype(BF)
        return carry

    lax.fori_loop(0, HEADS, turn, 0)
    for copy in w_copies:
        copy.wait()

    def sib_copy(block):
        return pltpu.make_async_remote_copy(
            src_ref=sibs.at[block], dst_ref=sibr.at[block],
            send_sem=sib_s.at[block], recv_sem=sib_r.at[block],
            device_id={"ctx": flipped(1)}, device_id_type=MESH,
        )

    def w_copy(to_chip, slot):
        return pltpu.make_async_remote_copy(
            src_ref=wsend.at[to_chip], dst_ref=wrecv.at[slot],
            send_sem=w_s.at[to_chip], recv_sem=w_r.at[slot],
            device_id={"ctx": to_chip * 2 + core}, device_id_type=MESH,
        )

    def block_terms(block, slot, first=False):
        def part(r, carry):
            at = rows_of(r * HALF, HALF)
            term = dot_nt(cotg[block, at, :], wb[block])
            gacc[at, :] = term if first else gacc[at, :] + term
            weight = dot(attnt[at, :], cotg[block])
            for m in range(4):
                wtile[m] = weight[:, m * DH : (m + 1) * DH]
            for i in range(2):
                wown[slot, i, at, :] = wtile[2 * i + core]
                sibs[block, i, at, :] = wtile[2 * i + 1 - core].astype(BF)
            return carry

        lax.fori_loop(0, 2, part, 0)
        sib_copy(block).start()

    def block_share(block, slot):
        sib_copy(block).wait_recv()
        for i in range(2):
            owner = 2 * block + i
            total = wown[slot, i] + sibr[block, i].astype(F32)

            @pl.when(owner == chip)
            def _():
                wmine[...] = total

            @pl.when(owner != chip)
            def _():
                wsend[owner] = total.astype(BF)
                w_copy(owner, chip).start()

    def nth_block(n):
        return (z + NZ + (1 - 2 * (n % 2)) * ((n + 1) // 2)) % NZ

    def blocks(first, last):
        def one(n, carry):
            block_terms(nth_block(n), n % 2)
            block_share(nth_block(n - 1), (n - 1) % 2)
            return carry

        lax.fori_loop(first, last, one, 0)

    block_terms(z, 0, first=True)
    ag_forward(3)
    blocks(1, 3)
    ag_forward(4)

    def mixed_part(block, chunk):
        return dot(attn[rows_of(chunk * HALF, HALF), :], wb[block])

    def rs_copy(d, i):
        return pltpu.make_async_remote_copy(
            src_ref=rss.at[d, i], dst_ref=rsr.at[d, i],
            send_sem=rs_s.at[d, i], recv_sem=rs_r.at[d, i],
            device_id={"head": (z + 1) % NZ if d == 0 else (z + NZ - 1) % NZ},
            device_id_type=MESH,
        )

    def rs_send(d, i, relay):
        distance = 4 - (i + 1) // 2
        block = (z + distance) % NZ if d == 0 else (z + NZ - distance) % NZ
        value = mixed_part(block, ag_chunk(d, i))
        if relay:
            rs_copy(d, i - 2).wait_recv()
            value = value + rsr[d, i - 2].astype(F32)
        rss[d, i] = value.astype(BF)
        rs_copy(d, i).start()

    def rs_relay(i):
        for d in range(2):
            rs_send(d, i + 2, True)

    for i in range(2):
        for d in range(2):
            rs_send(d, i, False)

    lmsib_copy.wait()
    lm2[...] = jnp.maximum(lmt[...], lmsib[...])

    def lm_copy(to_chip, slot):
        return pltpu.make_async_remote_copy(
            src_ref=lm2, dst_ref=lmr.at[slot], send_sem=lm_s.at[to_chip], recv_sem=lm_r.at[slot],
            device_id={"ctx": to_chip * 2 + core}, device_id_type=MESH,
        )

    def lm_start(j, carry):
        lm_copy((chip + j) % CHIPS, chip).start()
        return carry

    lax.fori_loop(1, CHIPS, lm_start, 0)

    blocks(3, 5)
    for d in range(2):
        ag_arrive(d, 5)
    blocks(5, 7)
    for d in range(2):
        ag_arrive(d, 6)
    blocks(7, 8)

    def permute_grad(b, carry):
        at = rows_of(b * BLK, BLK)
        gp[at, :] = dot(perm[...], gacc[at, :].astype(BF)).astype(BF)
        return carry

    lax.fori_loop(0, 4, permute_grad, 0)
    block_share(nth_block(7), 1)

    rsc, dq, rg = pk, tt, nm

    def score_grads(h, level, at, e, queries, keys, values):
        grad = rg[h, at, :].astype(BF)
        weights = dot_nt(grad, values)
        dz = (e * (weights - rsc[h, at, :][:, :1])).astype(BF)
        dq[h, at, :] = dot(dz, keys) * (SCALE * 0.5**level)
        return dot_tn(dz, queries) * SCALE, dot_tn(e.astype(BF), grad)

    def far_backward(h, carry):
        hs = lanes(h)

        def spread(b, inner):
            at = rows_of(b * BLK, BLK)
            g = gp[at, hs].astype(F32)
            delta = jnp.sum(g * af[h, at, :], axis=-1, keepdims=True)
            g = g.reshape(16, 8, DH)
            delta = jnp.broadcast_to(delta, (BLK, DH)).reshape(16, 8, DH)
            for level in range(LEVELS):
                share = wts5[h, level, at, :].reshape(16, 8, DH)
                grads, scalars = share * g, share * delta
                for _ in range(level):
                    grads, scalars = halve(grads), halve(scalars)
                n = BLK >> level
                put = rows_of(OFF[level] + b * n, n)
                rg[h, put, :] = grads.reshape(n, DH)
                rsc[h, put, :] = scalars.reshape(n, DH)
            return inner

        lax.fori_loop(0, 4, spread, 0)
        for level, queries, store in ((2, qc2, e2), (3, qc3, e3), (4, qc4, e4)):
            dk, dv = score_grads(
                h, level, pl.ds(OFF[level], TOK >> level), store[h],
                queries[:, hs], kvr[level - 2, 0, :, hs], kvr[level - 2, 1, :, hs],
            )
            gks[level - 2, 0, :, hs] = (dk * 0.5**level).astype(BF)
            gks[level - 2, 1, :, hs] = (dv * 0.5**level).astype(BF)
        return carry

    lax.fori_loop(0, HEADS, far_backward, 0)

    gk_sends = []
    for m in range(1, 8):
        if m == 1:
            src, dst, slot = gks.at[0], gkr2, 0
        elif m < 4:
            src = gks.at[1, :, rows_of(flipped(m) % 2 * 64, 64), :]
            dst, slot = gkr3.at[core], 1 + core
        else:
            src = gks.at[2, :, rows_of(flipped(m) % 4 * 32, 32), :]
            dst, slot = gkr4.at[c % 4], 3 + c % 4
        copy = pltpu.make_async_remote_copy(
            src_ref=src, dst_ref=dst, send_sem=gk_s.at[m], recv_sem=gk_r.at[slot],
            device_id={"ctx": flipped(m)}, device_id_type=MESH,
        )
        copy.start()
        gk_sends.append(copy)

    def near_backward(h, carry):
        hs = lanes(h)
        for p in range(2):
            at = pl.ds(p * 256, 256)
            dk, dv = score_grads(
                h, 0, at, e0[h, p], qkvp[0, at, hs], qkvp[1, at, hs], qkvp[2, at, hs]
            )
            gkp[at, hs] = dk
            gvp[at, hs] = dv
        for g in range(2):
            other = pl.ds((1 - g) * 128, 128)
            dk, dv = score_grads(
                h, 1, pl.ds(OFF[1] + g * 128, 128), e1[h, g],
                pool1[0, pl.ds(g * 128, 128), hs], pool1[1, other, hs], pool1[2, other, hs],
            )
            to = pl.ds((1 - g) * 256, 256)
            for ref, part in ((gkp, dk), (gvp, dv)):
                wide = expand((part * 0.5).reshape(16, 8, DH), 32).reshape(256, DH)
                ref[to, hs] = ref[to, hs] + wide

        def gather_q(b, inner):
            total = dq[h, rows_of(b * BLK, BLK), :].reshape(16, 8, DH)
            for level in range(1, LEVELS):
                n = BLK >> level
                part = dq[h, rows_of(OFF[level] + b * n, n), :].reshape(n // 8, 8, DH)
                total = total + expand(part, 16)
            gqp[rows_of(b * BLK, BLK), hs] = total.reshape(BLK, DH)
            return inner

        lax.fori_loop(0, 4, gather_q, 0)
        return carry

    rs_relay(0)
    lax.fori_loop(0, 2, near_backward, 0)
    rs_relay(1)
    lax.fori_loop(2, HEADS, near_backward, 0)
    rs_relay(2)

    def token_order(ref, b):
        at = rows_of(b * BLK, BLK)
        x = ref[at, :]
        high = x.astype(BF)
        low = (x - high.astype(F32)).astype(BF)
        ref[at, :] = dot(unperm[...], high) + dot(unperm[...], low)

    def finish_q(b, carry):
        token_order(gqp, b)
        return carry

    lax.fori_loop(0, 4, finish_q, 0)
    mix[pl.ds(0, HALF), :] = mixed_part(z, 0)
    mix[pl.ds(HALF, HALF), :] = mixed_part(z, 1)
    rs_relay(3)

    for slot in range(7):
        if slot == 0:
            src, dst = gks.at[0], gkr2
        elif slot < 3:
            src, dst = gks.at[1, :, pl.ds(0, 64), :], gkr3.at[slot - 1]
        else:
            src, dst = gks.at[2, :, pl.ds(0, 32), :], gkr4.at[slot - 3]
        pltpu.make_async_remote_copy(
            src_ref=src, dst_ref=dst, send_sem=gk_s.at[1], recv_sem=gk_r.at[slot],
            device_id={"ctx": flipped(1)}, device_id_type=MESH,
        ).wait_recv()

    for t, own in enumerate((gkp, gvp)):
        p4[t] = sum(gkr4[s, t].astype(F32) for s in range(4))

        def finish_kv(b, carry, t=t, own=own):
            at = rows_of(b * BLK, BLK)
            two = gkr2[t, rows_of(b * 32, 32), :].astype(F32)
            three = gkr3[0, t, rows_of(b * 16, 16), :].astype(F32)
            three = three + gkr3[1, t, rows_of(b * 16, 16), :].astype(F32)
            four = p4[t, rows_of(b * 8, 8), :]
            low = expand(three.reshape(2, 8, WID), 4) + expand(four.reshape(1, 8, WID), 4)
            low = low + two.reshape(4, 8, WID)
            own[at, :] = own[at, :] + expand(low, 16).reshape(BLK, WID)
            token_order(own, b)
            return carry

        lax.fori_loop(0, 4, finish_kv, 0)

    rs_relay(4)

    def w_sum(j, carry):
        slot = (chip + j) % CHIPS
        w_copy(chip, slot).wait_recv()
        wmine[...] = wmine[...] + wrecv[slot].astype(F32)
        return carry

    lax.fori_loop(1, CHIPS, w_sum, 0)

    def lm_max(j, carry):
        slot = (chip + j) % CHIPS
        lm_copy(chip, slot).wait_recv()
        lmt[...] = jnp.maximum(lmt[...], lmr[slot])
        return carry

    lmt[...] = lm2[...]
    lax.fori_loop(1, CHIPS, lm_max, 0)
    lm_out[...] = lmt[...][:HEADS, :LEVELS]

    for i, chunks in ((5, (1, 0)), (6, (0, 1))):
        for d in range(2):
            rs_copy(d, i).wait_recv()
            at = pl.ds(chunks[d] * HALF, HALF)
            mix[at, :] = mix[at, :] + rsr[d, i].astype(F32)

    for copy in kv_sends + gk_sends:
        copy.wait_send()

    def drain(i, carry):
        for d in range(2):
            ag_send(d, i).wait_send()
            rs_copy(d, i).wait_send()
        return carry

    lax.fori_loop(0, 7, drain, 0)

    def drain_sib(i, carry):
        sib_copy(i).wait_send()
        return carry

    lax.fori_loop(0, NZ, drain_sib, 0)

    def drain_chips(j, carry):
        to = (chip + j) % CHIPS
        w_copy(to, chip).wait_send()
        lm_copy(to, chip).wait_send()
        return carry

    lax.fori_loop(1, CHIPS, drain_chips, 0)


def finish(*refs):
    sems = refs[-1]
    copies = [pltpu.make_async_copy(refs[t], refs[6 + t], sems.at[t]) for t in range(6)]
    for copy in copies:
        copy.start()
    for copy in copies:
        copy.wait()


def vmem(shape, kind):
    return pltpu.VMEM(shape, kind)


def per_device(query_input, key_input, value_input, out_weight, out_cotangent):
    dma = pltpu.SemaphoreType.DMA
    scratch = [
        vmem((3, TOK, WID), BF),
        vmem((BLK, BLK), BF),
        vmem((BLK, BLK), BF),
        vmem((3, TOK, WID), BF),
        vmem((3, 256, WID), BF),
        vmem((128, WID), BF),
        vmem((64, WID), BF),
        vmem((3, 32, WID), F32),
        vmem((32, WID), BF),
        vmem((2, 128, WID), BF),
        vmem((2, 64, WID), BF),
        vmem((2, 32, WID), BF),
        vmem((3, 2, 128, WID), BF),
        vmem((HEADS, 2, 256, 256), F32),
        vmem((HEADS, 2, 128, 128), F32),
        vmem((HEADS, 128, 128), F32),
        vmem((HEADS, 64, 128), F32),
        vmem((HEADS, 32, 128), F32),
        vmem((HEADS, ROWS, DH), F32),
        vmem((HEADS, ROWS, DH), F32),
        vmem((HEADS, ROWS, DH), F32),
        vmem((HEADS, LEVELS, TOK, DH), F32),
        vmem((HEADS, TOK, DH), F32),
        vmem((TOK, WID), BF),
        vmem((TOK, WID), BF),
        vmem((WID, TOK), BF),
        vmem((NZ, TOK, WID), BF),
        vmem((NZ, WID, WID), BF),
        vmem((TOK, WID), F32),
        vmem((TOK, WID), BF),
        vmem((4, HALF, DH), F32),
        vmem((2, 2, WID, DH), F32),
        vmem((NZ, 2, WID, DH), BF),
        vmem((NZ, 2, WID, DH), BF),
        vmem((CHIPS, WID, DH), BF),
        vmem((CHIPS, WID, DH), BF),
        vmem((2, 7, HALF, WID), BF),
        vmem((2, 7, HALF, WID), BF),
        vmem((3, 2, 128, WID), BF),
        vmem((2, 128, WID), BF),
        vmem((2, 2, 64, WID), BF),
        vmem((4, 2, 32, WID), BF),
        vmem((8, DH), F32),
        vmem((8, DH), F32),
        vmem((8, DH), F32),
        vmem((CHIPS, 8, DH), F32),
        dma((3,)), dma((NZ,)), dma,
        dma((2, 7)), dma((2, 7)),
        dma((8,)), dma((7,)), dma((8,)), dma((7,)),
        dma((NZ,)), dma((NZ,)), dma((CHIPS,)), dma((CHIPS,)),
        dma((2, 7)), dma((2, 7)),
        dma, dma, dma((CHIPS,)), dma((CHIPS,)),
    ]
    outs = pl.pallas_call(
        kernel,
        out_shape=tuple(vmem((TOK, WID), F32) for _ in range(4))
        + (vmem((WID, DH), F32), vmem((HEADS, LEVELS), F32)),
        in_specs=[pl.BlockSpec(memory_space=pl.ANY)] * 5,
        out_specs=[pl.BlockSpec(memory_space=pltpu.VMEM)] * 6,
        scratch_shapes=scratch,
        compiler_params=pltpu.CompilerParams(
            collective_id=0, has_side_effects=True, vmem_limit_bytes=56000000
        ),
        name="layer",
    )(query_input, key_input, value_input, out_weight, out_cotangent)
    held = [pltpu.with_memory_space_constraint(x, pltpu.VMEM) for x in outs]
    anywhere = pl.BlockSpec(memory_space=pl.ANY)
    local = pl.BlockSpec(memory_space=pltpu.VMEM)
    wide = jax.ShapeDtypeStruct((TOK, WID), F32)
    outs = pl.pallas_call(
        finish,
        out_shape=(
            wide, wide, wide, wide,
            jax.ShapeDtypeStruct((WID, DH), F32),
            jax.ShapeDtypeStruct((HEADS, LEVELS), F32),
        ),
        in_specs=[local] * 6,
        out_specs=[anywhere] * 6,
        scratch_shapes=[dma((6,))],
        compiler_params=pltpu.CompilerParams(vmem_limit_bytes=1000000),
        name="finish",
    )(*held)
    return outs[:5] + (outs[5].T,)


def solution(mesh):
    in_specs = (
        P("ctx", "head"),
        P("ctx", "head"),
        P("ctx", "head"),
        P("head", None),
        P("ctx", "head"),
    )
    out_specs = (
        P("ctx", "head"),
        P("ctx", "head"),
        P("ctx", "head"),
        P("ctx", "head"),
        P("head", "ctx"),
        P(None, "head"),
    )
    return jax.shard_map(
        per_device, mesh=mesh, in_specs=in_specs, out_specs=out_specs, check_vma=False
    )
```

```python
import functools
import math

import jax
import jax.numpy as jnp
from jax import lax
from jax.experimental import pallas as pl
from jax.experimental.pallas import tpu as pltpu
from jax.sharding import PartitionSpec as P

DH = 128
BLK = 128
LEVELS = 5
NZ = 8
NCTX = 32
CHIPS = 16
HEADS = 4
TOK = 512
WID = HEADS * DH
HALF = TOK // 2
LOG_TWO = math.log(2.0)
SCALE = DH ** (-0.5)
MESH = pl.DeviceIdType.MESH
BF = jnp.bfloat16
F32 = jnp.float32
OFF = (0, 512, 768, 896, 960)
ROWS = 992


def dot(a, b):
    return lax.dot_general(a, b, (((1,), (0,)), ((), ())), preferred_element_type=F32)


def dot_nt(a, b):
    return lax.dot_general(a, b, (((1,), (1,)), ((), ())), preferred_element_type=F32)


def dot_tn(a, b):
    return lax.dot_general(a, b, (((0,), (0,)), ((), ())), preferred_element_type=F32)


def rows_of(start, size):
    return pl.ds(pl.multiple_of(start, size), size)


def expand(x, slabs):
    n = x.shape[0]
    if n == slabs:
        return x
    return jnp.broadcast_to(x[:, None], (n, slabs // n, 8, x.shape[2])).reshape(
        slabs, 8, x.shape[2]
    )


def halve(x):
    y = x.reshape(x.shape[0] // 2, 2, 8, x.shape[2])
    return y[:, 0] + y[:, 1]


def kernel(
    q_in, k_in, v_in, w_in, c_in,
    mix, gqp, gkp, gvp, wmine, lm_out,
    qkv, perm, unperm, qkvp, pool1, qc2, qc3, p4, qc4, kvs2, kvs3, kvs4, kvr,
    e0, e1, e2, e3, e4, pk, tt, nm, wts5, af, ap, attn, attnt,
    cotg, wb, gacc, gp, wtile, wown, sibs, sibr, wsend, wrecv, wrow, ysend, yrecv,
    rss, rsr, gks, gkr2, gkr3, gkr4, lmt, lmsib, lm2, lmr,
    in_sem, w_sem, c_sem, ag_s, ag_r, kv_s, kv_r, gk_s, gk_r,
    sib_s, sib_r, w_s, w_r, y_s, y_r, rs_s, rs_r, lmsib_s, lmsib_r, lm_s, lm_r,
):
    c = lax.axis_index("ctx")
    z = lax.axis_index("head")
    core = c % 2
    chip = c // 2
    x_here, y_here = chip % 4, chip // 4

    def flipped(m):
        out = c
        for bit in range(3):
            if m >> bit & 1:
                out = out + (1 - 2 * (c // 2**bit % 2)) * 2**bit
        return out

    c_copy = pltpu.make_async_copy(c_in, cotg.at[z], c_sem)
    c_copy.start()
    in_copies = [
        pltpu.make_async_copy(src, qkv.at[t], in_sem.at[t])
        for t, src in enumerate((q_in, k_in, v_in))
    ]
    for copy in in_copies:
        copy.start()
    w_copies = [
        pltpu.make_async_copy(w_in.at[:, pl.ds(j * WID, WID)], wb.at[j], w_sem.at[j])
        for j in range(NZ)
    ]
    for copy in w_copies:
        copy.start()

    barrier = pltpu.get_barrier_semaphore()
    for step in (1, NZ - 1):
        pl.semaphore_signal(
            barrier, inc=1, device_id={"head": (z + step) % NZ}, device_id_type=MESH
        )
    for m in range(1, 8):
        pl.semaphore_signal(barrier, inc=1, device_id={"ctx": flipped(m)}, device_id_type=MESH)

    def greet(j, carry):
        pl.semaphore_signal(
            barrier,
            inc=1,
            device_id={"ctx": (chip + j) % CHIPS * 2 + core},
            device_id_type=MESH,
        )
        return carry

    lax.fori_loop(1, CHIPS, greet, 0)
    pl.semaphore_wait(barrier, 2 + 7 + CHIPS - 1)

    def ag_region(d, block, chunk):
        return cotg.at[block, rows_of(chunk * HALF, HALF), :]

    def ag_chunk(d, i):
        return i % 2 if d == 0 else 1 - i % 2

    def ag_send(d, i):
        if d == 0:
            block, to = (z + NZ - i // 2) % NZ, (z + 1) % NZ
        else:
            block, to = (z + i // 2) % NZ, (z + NZ - 1) % NZ
        region = ag_region(d, block, ag_chunk(d, i))
        return pltpu.make_async_remote_copy(
            src_ref=region, dst_ref=region, send_sem=ag_s.at[d, i], recv_sem=ag_r.at[d, i],
            device_id={"head": to}, device_id_type=MESH,
        )

    def ag_arrive(d, i):
        if d == 0:
            block = (z + 2 * NZ - 1 - i // 2) % NZ
        else:
            block = (z + 1 + i // 2) % NZ
        region = ag_region(d, block, ag_chunk(d, i))
        pltpu.make_async_remote_copy(
            src_ref=region, dst_ref=region, send_sem=ag_s.at[d, i], recv_sem=ag_r.at[d, i],
            device_id={"head": (z + 1) % NZ}, device_id_type=MESH,
        ).wait_recv()

    def ag_forward(i):
        for d in range(2):
            ag_arrive(d, i)
            ag_send(d, i + 2).start()

    c_copy.wait()
    for i in range(2):
        for d in range(2):
            ag_send(d, i).start()

    row_id = lax.broadcasted_iota(jnp.int32, (BLK, BLK), 0)
    col_id = lax.broadcasted_iota(jnp.int32, (BLK, BLK), 1)
    perm[...] = jnp.where(col_id == row_id % 8 * 16 + row_id // 8, 1.0, 0.0).astype(BF)
    unperm[...] = jnp.where(row_id == col_id % 8 * 16 + col_id // 8, 1.0, 0.0).astype(BF)
    lmt[...] = jnp.full((8, DH), -3.0e38, F32)

    for t in (1, 2, 0):
        in_copies[t].wait()

        def pool(b, carry, t=t):
            x = dot(perm[...], qkv[t, rows_of(b * BLK, BLK), :])
            qkvp[t, rows_of(b * BLK, BLK), :] = x.astype(BF)
            one = halve(x.reshape(16, 8, WID))
            pool1[t, rows_of(b * 64, 64), :] = (one * 0.5).reshape(64, WID).astype(BF)
            two = halve(one)
            two_rows = (two * 0.25).reshape(32, WID).astype(BF)
            three = halve(two)
            three_rows = (three * 0.125).reshape(16, WID).astype(BF)
            if t == 0:
                qc2[rows_of(b * 32, 32), :] = two_rows
                qc3[rows_of(b * 16, 16), :] = three_rows
            else:
                kvs2[t - 1, rows_of(b * 32, 32), :] = two_rows
                kvs3[t - 1, rows_of(b * 16, 16), :] = three_rows
            p4[t, rows_of(b * 8, 8), :] = (halve(three) * 0.0625).reshape(8, WID)
            return carry

        lax.fori_loop(0, 4, pool, 0)
        if t == 0:
            qc4[...] = p4[0].astype(BF)
        else:
            kvs4[t - 1] = p4[t].astype(BF)

        if t == 2:
            kv_sends = []
            for m in range(1, 8):
                if m == 1:
                    src, dst, slot = kvs2, kvr.at[0], 0
                elif m < 4:
                    src, slot = kvs3, 1 + core
                    dst = kvr.at[1, :, rows_of(core * 64, 64), :]
                else:
                    src, slot = kvs4, 3 + c % 4
                    dst = kvr.at[2, :, rows_of(c % 4 * 32, 32), :]
                copy = pltpu.make_async_remote_copy(
                    src_ref=src, dst_ref=dst, send_sem=kv_s.at[m], recv_sem=kv_r.at[slot],
                    device_id={"ctx": flipped(m)}, device_id_type=MESH,
                )
                copy.start()
                kv_sends.append(copy)

    def kv_arrive():
        for slot in range(7):
            if slot == 0:
                src, dst = kvs2, kvr.at[0]
            elif slot < 3:
                src, dst = kvs3, kvr.at[1, :, pl.ds((slot - 1) * 64, 64), :]
            else:
                src, dst = kvs4, kvr.at[2, :, pl.ds((slot - 3) * 32, 32), :]
            pltpu.make_async_remote_copy(
                src_ref=src, dst_ref=dst, send_sem=kv_s.at[1], recv_sem=kv_r.at[slot],
                device_id={"ctx": flipped(1)}, device_id_type=MESH,
            ).wait_recv()

    tile_row = lax.broadcasted_iota(jnp.int32, (8, DH), 0)
    tile_col = lax.broadcasted_iota(jnp.int32, (8, DH), 1)

    def attend(h, level, start, count, queries, keys, values):
        scores = dot_nt(queries, keys) * SCALE
        peak = jnp.max(scores, axis=-1, keepdims=True)
        e = jnp.exp(scores - peak)
        total = jnp.sum(e, axis=-1, keepdims=True)
        wide = jnp.broadcast_to(peak, (count, DH))
        at = pl.ds(start, count) if isinstance(start, int) else start
        pk[h, at, :] = wide + level * LOG_TWO
        tt[h, at, :] = jnp.broadcast_to(total, (count, DH))
        nm[h, at, :] = dot(e.astype(BF), values)
        top = jnp.max(wide.reshape(count // 8, 8, DH), axis=0)
        top = jnp.broadcast_to(jnp.max(top, axis=0, keepdims=True), (8, DH))
        here = jnp.logical_and(tile_row == h, tile_col == level)
        lmt[...] = jnp.where(here, jnp.maximum(lmt[...], top), lmt[...])
        return e

    def lanes(h):
        return rows_of(h * DH, DH)

    def near_forward(h, carry):
        hs = lanes(h)
        for p in range(2):
            at = pl.ds(p * 256, 256)
            e0[h, p] = attend(h, 0, p * 256, 256, qkvp[0, at, hs], qkvp[1, at, hs], qkvp[2, at, hs])
        for g in range(2):
            other = pl.ds((1 - g) * 128, 128)
            e1[h, g] = attend(
                h, 1, OFF[1] + g * 128, 128,
                pool1[0, pl.ds(g * 128, 128), hs], pool1[1, other, hs], pool1[2, other, hs],
            )
        return carry

    lax.fori_loop(0, HEADS, near_forward, 0)
    ag_forward(0)
    ag_forward(1)
    kv_arrive()

    def far_forward(h, carry):
        hs = lanes(h)
        for level, queries, store in ((2, qc2, e2), (3, qc3, e3), (4, qc4, e4)):
            count = TOK >> level
            store[h] = attend(
                h, level, OFF[level], count,
                queries[:, hs], kvr[level - 2, 0, :, hs], kvr[level - 2, 1, :, hs],
            )

        def merge(b, inner):
            def level_rows(ref, level):
                n = BLK >> level
                return expand(ref[h, rows_of(OFF[level] + b * n, n), :].reshape(n // 8, 8, DH), 16)

            peaks = [level_rows(pk, level) for level in range(LEVELS)]
            highest = peaks[0]
            for other in peaks[1:]:
                highest = jnp.maximum(highest, other)
            scales = [jnp.exp(peak - highest) for peak in peaks]
            den = scales[0] * level_rows(tt, 0)
            num = scales[0] * level_rows(nm, 0)
            for level in range(1, LEVELS):
                den = den + scales[level] * level_rows(tt, level)
                num = num + scales[level] * level_rows(nm, level)
            inv = 1.0 / den
            at = rows_of(b * BLK, BLK)
            for level in range(LEVELS):
                wts5[h, level, at, :] = (scales[level] * inv).reshape(BLK, DH)
            out = (num * inv).reshape(BLK, DH)
            af[h, at, :] = out
            ap[at, hs] = out.astype(BF)
            return inner

        lax.fori_loop(0, 4, merge, 0)
        return carry

    lax.fori_loop(0, HEADS, far_forward, 0)
    ag_forward(2)

    lmsib_copy = pltpu.make_async_remote_copy(
        src_ref=lmt, dst_ref=lmsib, send_sem=lmsib_s, recv_sem=lmsib_r,
        device_id={"ctx": flipped(1)}, device_id_type=MESH,
    )
    lmsib_copy.start()

    def restore(b, carry):
        at = rows_of(b * BLK, BLK)
        attn[at, :] = dot(unperm[...], ap[at, :]).astype(BF)
        return carry

    lax.fori_loop(0, 4, restore, 0)

    def turn(f, carry):
        attnt[rows_of(f * DH, DH), :] = attn[:, rows_of(f * DH, DH)].astype(F32).T.astype(BF)
        return carry

    lax.fori_loop(0, HEADS, turn, 0)
    for copy in w_copies:
        copy.wait()

    def sib_copy(block):
        return pltpu.make_async_remote_copy(
            src_ref=sibs.at[block], dst_ref=sibr.at[block],
            send_sem=sib_s.at[block], recv_sem=sib_r.at[block],
            device_id={"ctx": flipped(1)}, device_id_type=MESH,
        )

    def x_copy(owner, sender):
        return pltpu.make_async_remote_copy(
            src_ref=wsend.at[owner], dst_ref=wrecv.at[owner // 4, sender],
            send_sem=w_s.at[owner], recv_sem=w_r.at[owner // 4, sender],
            device_id={"ctx": (y_here * 4 + owner % 4) * 2 + core}, device_id_type=MESH,
        )

    def y_copy(to_y, sender):
        return pltpu.make_async_remote_copy(
            src_ref=ysend.at[to_y], dst_ref=yrecv.at[sender],
            send_sem=y_s.at[to_y], recv_sem=y_r.at[sender],
            device_id={"ctx": (to_y * 4 + x_here) * 2 + core}, device_id_type=MESH,
        )

    def block_terms(block, slot, first=False):
        def part(r, carry):
            at = rows_of(r * HALF, HALF)
            term = dot_nt(cotg[block, at, :], wb[block])
            gacc[at, :] = term if first else gacc[at, :] + term
            weight = dot(attnt[at, :], cotg[block])
            for m in range(4):
                wtile[m] = weight[:, m * DH : (m + 1) * DH]
            for i in range(2):
                wown[slot, i, at, :] = wtile[2 * i + core]
                sibs[block, i, at, :] = wtile[2 * i + 1 - core].astype(BF)
            return carry

        lax.fori_loop(0, 2, part, 0)
        sib_copy(block).start()

    def block_share(block, slot):
        sib_copy(block).wait_recv()
        for i in range(2):
            owner = 2 * block + i
            total = wown[slot, i] + sibr[block, i].astype(F32)

            @pl.when(owner % 4 == x_here)
            def _():
                wrow[owner // 4] = total

            @pl.when(owner % 4 != x_here)
            def _():
                wsend[owner] = total.astype(BF)
                x_copy(owner, x_here).start()

    def row_share(block):
        to_y = block // 2

        @pl.when(block % 2 == x_here // 2)
        def _():
            for j in range(1, 4):
                sender = (x_here + j) % 4
                x_copy(to_y * 4 + x_here, sender).wait_recv()
            total = wrow[to_y]
            for j in range(1, 4):
                total = total + wrecv[to_y, (x_here + j) % 4].astype(F32)

            @pl.when(to_y == y_here)
            def _():
                wmine[...] = total

            @pl.when(to_y != y_here)
            def _():
                ysend[to_y] = total.astype(BF)
                y_copy(to_y, y_here).start()

    def nth_block(n):
        return (z + NZ + (1 - 2 * (n % 2)) * ((n + 1) // 2)) % NZ

    def blocks(first, last):
        def one(n, carry):
            block_terms(nth_block(n), n % 2)
            block_share(nth_block(n - 1), (n - 1) % 2)
            return carry

        lax.fori_loop(first, last, one, 0)

    block_terms(z, 0, first=True)
    ag_forward(3)
    blocks(1, 3)
    ag_forward(4)

    def mixed_part(block, chunk):
        return dot(attn[rows_of(chunk * HALF, HALF), :], wb[block])

    def rs_copy(d, i):
        return pltpu.make_async_remote_copy(
            src_ref=rss.at[d, i], dst_ref=rsr.at[d, i],
            send_sem=rs_s.at[d, i], recv_sem=rs_r.at[d, i],
            device_id={"head": (z + 1) % NZ if d == 0 else (z + NZ - 1) % NZ},
            device_id_type=MESH,
        )

    def rs_send(d, i, relay):
        distance = 4 - (i + 1) // 2
        block = (z + distance) % NZ if d == 0 else (z + NZ - distance) % NZ
        value = mixed_part(block, ag_chunk(d, i))
        if relay:
            rs_copy(d, i - 2).wait_recv()
            value = value + rsr[d, i - 2].astype(F32)
        rss[d, i] = value.astype(BF)
        rs_copy(d, i).start()

    def rs_relay(i):
        for d in range(2):
            rs_send(d, i + 2, True)

    for i in range(2):
        for d in range(2):
            rs_send(d, i, False)

    lmsib_copy.wait()
    lm2[...] = jnp.maximum(lmt[...], lmsib[...])

    def lm_copy(to_chip, slot):
        return pltpu.make_async_remote_copy(
            src_ref=lm2, dst_ref=lmr.at[slot], send_sem=lm_s.at[to_chip], recv_sem=lm_r.at[slot],
            device_id={"ctx": to_chip * 2 + core}, device_id_type=MESH,
        )

    def lm_start(j, carry):
        lm_copy((chip + j) % CHIPS, chip).start()
        return carry

    lax.fori_loop(1, CHIPS, lm_start, 0)

    blocks(3, 5)
    for d in range(2):
        ag_arrive(d, 5)
    blocks(5, 7)
    for d in range(2):
        ag_arrive(d, 6)
    blocks(7, 8)

    def permute_grad(b, carry):
        at = rows_of(b * BLK, BLK)
        gp[at, :] = dot(perm[...], gacc[at, :].astype(BF)).astype(BF)
        return carry

    lax.fori_loop(0, 4, permute_grad, 0)
    block_share(nth_block(7), 1)

    rsc, dq, rg = pk, tt, nm

    def score_grads(h, level, at, e, queries, keys, values):
        grad = rg[h, at, :].astype(BF)
        weights = dot_nt(grad, values)
        dz = (e * (weights - rsc[h, at, :][:, :1])).astype(BF)
        dq[h, at, :] = dot(dz, keys) * (SCALE * 0.5**level)
        return dot_tn(dz, queries) * SCALE, dot_tn(e.astype(BF), grad)

    def far_backward(h, carry):
        hs = lanes(h)

        def spread(b, inner):
            at = rows_of(b * BLK, BLK)
            g = gp[at, hs].astype(F32)
            delta = jnp.sum(g * af[h, at, :], axis=-1, keepdims=True)
            g = g.reshape(16, 8, DH)
            delta = jnp.broadcast_to(delta, (BLK, DH)).reshape(16, 8, DH)
            for level in range(LEVELS):
                share = wts5[h, level, at, :].reshape(16, 8, DH)
                grads, scalars = share * g, share * delta
                for _ in range(level):
                    grads, scalars = halve(grads), halve(scalars)
                n = BLK >> level
                put = rows_of(OFF[level] + b * n, n)
                rg[h, put, :] = grads.reshape(n, DH)
                rsc[h, put, :] = scalars.reshape(n, DH)
            return inner

        lax.fori_loop(0, 4, spread, 0)
        for level, queries, store in ((2, qc2, e2), (3, qc3, e3), (4, qc4, e4)):
            dk, dv = score_grads(
                h, level, pl.ds(OFF[level], TOK >> level), store[h],
                queries[:, hs], kvr[level - 2, 0, :, hs], kvr[level - 2, 1, :, hs],
            )
            gks[level - 2, 0, :, hs] = (dk * 0.5**level).astype(BF)
            gks[level - 2, 1, :, hs] = (dv * 0.5**level).astype(BF)
        return carry

    lax.fori_loop(0, HEADS, far_backward, 0)

    gk_sends = []
    for m in range(1, 8):
        if m == 1:
            src, dst, slot = gks.at[0], gkr2, 0
        elif m < 4:
            src = gks.at[1, :, rows_of(flipped(m) % 2 * 64, 64), :]
            dst, slot = gkr3.at[core], 1 + core
        else:
            src = gks.at[2, :, rows_of(flipped(m) % 4 * 32, 32), :]
            dst, slot = gkr4.at[c % 4], 3 + c % 4
        copy = pltpu.make_async_remote_copy(
            src_ref=src, dst_ref=dst, send_sem=gk_s.at[m], recv_sem=gk_r.at[slot],
            device_id={"ctx": flipped(m)}, device_id_type=MESH,
        )
        copy.start()
        gk_sends.append(copy)

    def near_backward(h, carry):
        hs = lanes(h)
        for p in range(2):
            at = pl.ds(p * 256, 256)
            dk, dv = score_grads(
                h, 0, at, e0[h, p], qkvp[0, at, hs], qkvp[1, at, hs], qkvp[2, at, hs]
            )
            gkp[at, hs] = dk
            gvp[at, hs] = dv
        for g in range(2):
            other = pl.ds((1 - g) * 128, 128)
            dk, dv = score_grads(
                h, 1, pl.ds(OFF[1] + g * 128, 128), e1[h, g],
                pool1[0, pl.ds(g * 128, 128), hs], pool1[1, other, hs], pool1[2, other, hs],
            )
            to = pl.ds((1 - g) * 256, 256)
            for ref, part in ((gkp, dk), (gvp, dv)):
                wide = expand((part * 0.5).reshape(16, 8, DH), 32).reshape(256, DH)
                ref[to, hs] = ref[to, hs] + wide

        def gather_q(b, inner):
            total = dq[h, rows_of(b * BLK, BLK), :].reshape(16, 8, DH)
            for level in range(1, LEVELS):
                n = BLK >> level
                part = dq[h, rows_of(OFF[level] + b * n, n), :].reshape(n // 8, 8, DH)
                total = total + expand(part, 16)
            gqp[rows_of(b * BLK, BLK), hs] = total.reshape(BLK, DH)
            return inner

        lax.fori_loop(0, 4, gather_q, 0)
        return carry

    def row_shares(first, last):
        def one(n, carry):
            row_share(nth_block(n))
            return carry

        lax.fori_loop(first, last, one, 0)

    rs_relay(0)
    lax.fori_loop(0, 2, near_backward, 0)
    rs_relay(1)
    row_shares(0, 3)
    lax.fori_loop(2, HEADS, near_backward, 0)
    rs_relay(2)
    row_shares(3, 7)

    def token_order(ref, b):
        at = rows_of(b * BLK, BLK)
        x = ref[at, :]
        high = x.astype(BF)
        low = (x - high.astype(F32)).astype(BF)
        ref[at, :] = dot(unperm[...], high) + dot(unperm[...], low)

    def finish_q(b, carry):
        token_order(gqp, b)
        return carry

    lax.fori_loop(0, 4, finish_q, 0)
    mix[pl.ds(0, HALF), :] = mixed_part(z, 0)
    mix[pl.ds(HALF, HALF), :] = mixed_part(z, 1)
    rs_relay(3)
    row_shares(7, 8)

    for slot in range(7):
        if slot == 0:
            src, dst = gks.at[0], gkr2
        elif slot < 3:
            src, dst = gks.at[1, :, pl.ds(0, 64), :], gkr3.at[slot - 1]
        else:
            src, dst = gks.at[2, :, pl.ds(0, 32), :], gkr4.at[slot - 3]
        pltpu.make_async_remote_copy(
            src_ref=src, dst_ref=dst, send_sem=gk_s.at[1], recv_sem=gk_r.at[slot],
            device_id={"ctx": flipped(1)}, device_id_type=MESH,
        ).wait_recv()

    for t, own in enumerate((gkp, gvp)):
        p4[t] = sum(gkr4[s, t].astype(F32) for s in range(4))

        def finish_kv(b, carry, t=t, own=own):
            at = rows_of(b * BLK, BLK)
            two = gkr2[t, rows_of(b * 32, 32), :].astype(F32)
            three = gkr3[0, t, rows_of(b * 16, 16), :].astype(F32)
            three = three + gkr3[1, t, rows_of(b * 16, 16), :].astype(F32)
            four = p4[t, rows_of(b * 8, 8), :]
            low = expand(three.reshape(2, 8, WID), 4) + expand(four.reshape(1, 8, WID), 4)
            low = low + two.reshape(4, 8, WID)
            own[at, :] = own[at, :] + expand(low, 16).reshape(BLK, WID)
            token_order(own, b)
            return carry

        lax.fori_loop(0, 4, finish_kv, 0)

    rs_relay(4)

    for j in range(1, 4):
        y_copy(y_here, (y_here + j) % 4).wait_recv()
    total = wmine[...]
    for j in range(1, 4):
        total = total + yrecv[(y_here + j) % 4].astype(F32)
    wmine[...] = total

    def lm_max(j, carry):
        slot = (chip + j) % CHIPS
        lm_copy(chip, slot).wait_recv()
        lmt[...] = jnp.maximum(lmt[...], lmr[slot])
        return carry

    lmt[...] = lm2[...]
    lax.fori_loop(1, CHIPS, lm_max, 0)
    lm_out[...] = lmt[...][:HEADS, :LEVELS]

    for i, chunks in ((5, (1, 0)), (6, (0, 1))):
        for d in range(2):
            rs_copy(d, i).wait_recv()
            at = pl.ds(chunks[d] * HALF, HALF)
            mix[at, :] = mix[at, :] + rsr[d, i].astype(F32)

    for copy in kv_sends + gk_sends:
        copy.wait_send()

    def drain(i, carry):
        for d in range(2):
            ag_send(d, i).wait_send()
            rs_copy(d, i).wait_send()
        return carry

    lax.fori_loop(0, 7, drain, 0)

    def drain_sib(i, carry):
        sib_copy(i).wait_send()
        return carry

    lax.fori_loop(0, NZ, drain_sib, 0)

    def drain_chips(j, carry):
        to = (chip + j) % CHIPS
        lm_copy(to, chip).wait_send()

        @pl.when(to % 4 != x_here)
        def _():
            x_copy(to, x_here).wait_send()

        return carry

    lax.fori_loop(1, CHIPS, drain_chips, 0)
    for j in range(1, 4):
        y_copy((y_here + j) % 4, y_here).wait_send()


def finish(*refs):
    sems = refs[-1]
    copies = [pltpu.make_async_copy(refs[t], refs[6 + t], sems.at[t]) for t in range(6)]
    for copy in copies:
        copy.start()
    for copy in copies:
        copy.wait()


def vmem(shape, kind):
    return pltpu.VMEM(shape, kind)


def per_device(query_input, key_input, value_input, out_weight, out_cotangent):
    dma = pltpu.SemaphoreType.DMA
    scratch = [
        vmem((3, TOK, WID), BF),
        vmem((BLK, BLK), BF),
        vmem((BLK, BLK), BF),
        vmem((3, TOK, WID), BF),
        vmem((3, 256, WID), BF),
        vmem((128, WID), BF),
        vmem((64, WID), BF),
        vmem((3, 32, WID), F32),
        vmem((32, WID), BF),
        vmem((2, 128, WID), BF),
        vmem((2, 64, WID), BF),
        vmem((2, 32, WID), BF),
        vmem((3, 2, 128, WID), BF),
        vmem((HEADS, 2, 256, 256), F32),
        vmem((HEADS, 2, 128, 128), F32),
        vmem((HEADS, 128, 128), F32),
        vmem((HEADS, 64, 128), F32),
        vmem((HEADS, 32, 128), F32),
        vmem((HEADS, ROWS, DH), F32),
        vmem((HEADS, ROWS, DH), F32),
        vmem((HEADS, ROWS, DH), F32),
        vmem((HEADS, LEVELS, TOK, DH), F32),
        vmem((HEADS, TOK, DH), F32),
        vmem((TOK, WID), BF),
        vmem((TOK, WID), BF),
        vmem((WID, TOK), BF),
        vmem((NZ, TOK, WID), BF),
        vmem((NZ, WID, WID), BF),
        vmem((TOK, WID), F32),
        vmem((TOK, WID), BF),
        vmem((4, HALF, DH), F32),
        vmem((2, 2, WID, DH), F32),
        vmem((NZ, 2, WID, DH), BF),
        vmem((NZ, 2, WID, DH), BF),
        vmem((CHIPS, WID, DH), BF),
        vmem((4, 4, WID, DH), BF),
        vmem((4, WID, DH), F32),
        vmem((4, WID, DH), BF),
        vmem((4, WID, DH), BF),
        vmem((2, 7, HALF, WID), BF),
        vmem((2, 7, HALF, WID), BF),
        vmem((3, 2, 128, WID), BF),
        vmem((2, 128, WID), BF),
        vmem((2, 2, 64, WID), BF),
        vmem((4, 2, 32, WID), BF),
        vmem((8, DH), F32),
        vmem((8, DH), F32),
        vmem((8, DH), F32),
        vmem((CHIPS, 8, DH), F32),
        dma((3,)), dma((NZ,)), dma,
        dma((2, 7)), dma((2, 7)),
        dma((8,)), dma((7,)), dma((8,)), dma((7,)),
        dma((NZ,)), dma((NZ,)), dma((CHIPS,)), dma((4, 4)), dma((4,)), dma((4,)),
        dma((2, 7)), dma((2, 7)),
        dma, dma, dma((CHIPS,)), dma((CHIPS,)),
    ]
    outs = pl.pallas_call(
        kernel,
        out_shape=tuple(vmem((TOK, WID), F32) for _ in range(4))
        + (vmem((WID, DH), F32), vmem((HEADS, LEVELS), F32)),
        in_specs=[pl.BlockSpec(memory_space=pl.ANY)] * 5,
        out_specs=[pl.BlockSpec(memory_space=pltpu.VMEM)] * 6,
        scratch_shapes=scratch,
        compiler_params=pltpu.CompilerParams(
            collective_id=0, has_side_effects=True, vmem_limit_bytes=56000000
        ),
        name="layer",
    )(query_input, key_input, value_input, out_weight, out_cotangent)
    held = [pltpu.with_memory_space_constraint(x, pltpu.VMEM) for x in outs]
    anywhere = pl.BlockSpec(memory_space=pl.ANY)
    local = pl.BlockSpec(memory_space=pltpu.VMEM)
    wide = jax.ShapeDtypeStruct((TOK, WID), F32)
    outs = pl.pallas_call(
        finish,
        out_shape=(
            wide, wide, wide, wide,
            jax.ShapeDtypeStruct((WID, DH), F32),
            jax.ShapeDtypeStruct((HEADS, LEVELS), F32),
        ),
        in_specs=[local] * 6,
        out_specs=[anywhere] * 6,
        scratch_shapes=[dma((6,))],
        compiler_params=pltpu.CompilerParams(vmem_limit_bytes=1000000),
        name="finish",
    )(*held)
    return outs[:5] + (outs[5].T,)


def solution(mesh):
    in_specs = (
        P("ctx", "head"),
        P("ctx", "head"),
        P("ctx", "head"),
        P("head", None),
        P("ctx", "head"),
    )
    out_specs = (
        P("ctx", "head"),
        P("ctx", "head"),
        P("ctx", "head"),
        P("ctx", "head"),
        P("head", "ctx"),
        P(None, "head"),
    )
    return jax.shard_map(
        per_device, mesh=mesh, in_specs=in_specs, out_specs=out_specs, check_vma=False
    )
```

```python
import functools
import math

import jax
import jax.numpy as jnp
from jax import lax
from jax.experimental import pallas as pl
from jax.experimental.pallas import tpu as pltpu
from jax.sharding import PartitionSpec as P

DH = 128
BLK = 128
LEVELS = 5
NZ = 8
NCTX = 32
CHIPS = 16
HEADS = 4
TOK = 512
WID = HEADS * DH
HALF = TOK // 2
LOG_TWO = math.log(2.0)
SCALE = DH ** (-0.5)
MESH = pl.DeviceIdType.MESH
BF = jnp.bfloat16
F32 = jnp.float32
OFF = (0, 512, 768, 896, 960)
ROWS = 992


def dot(a, b):
    return lax.dot_general(a, b, (((1,), (0,)), ((), ())), preferred_element_type=F32)


def dot_nt(a, b):
    return lax.dot_general(a, b, (((1,), (1,)), ((), ())), preferred_element_type=F32)


def dot_tn(a, b):
    return lax.dot_general(a, b, (((0,), (0,)), ((), ())), preferred_element_type=F32)


def rows_of(start, size):
    return pl.ds(pl.multiple_of(start, size), size)


def expand(x, slabs):
    n = x.shape[0]
    if n == slabs:
        return x
    return jnp.broadcast_to(x[:, None], (n, slabs // n, 8, x.shape[2])).reshape(
        slabs, 8, x.shape[2]
    )


def halve(x):
    y = x.reshape(x.shape[0] // 2, 2, 8, x.shape[2])
    return y[:, 0] + y[:, 1]


def kernel(
    q_in, k_in, v_in, w_in, c_in,
    mix, gqp, gkp, gvp, wmine, lm_out,
    qkv, perm, unperm, qkvp, pool1, qc2, qc3, p4, qc4, kvs2, kvs3, kvs4, kvr,
    e0, e1, e2, e3, e4, pk, tt, nm, wts5, af, ap, attn, attnt,
    cotg, wb, gacc, gp, wtile, wown, sibs, sibr, wsend, wrecv, wrow, ysend, yrecv,
    rss, rsr, held, gks, gkr2, gkr3, gkr4, lmt, lmsib, lm2, lmr,
    in_sem, w_sem, c_sem, ag_s, ag_r, kv_s, kv_r, gk_s, gk_r,
    sib_s, sib_r, w_s, w_r, y_s, y_r, rs_s, rs_r, lmsib_s, lmsib_r, lm_s, lm_r,
):
    c = lax.axis_index("ctx")
    z = lax.axis_index("head")
    core = c % 2
    chip = c // 2
    x_here, y_here = chip % 4, chip // 4

    def flipped(m):
        out = c
        for bit in range(3):
            if m >> bit & 1:
                out = out + (1 - 2 * (c // 2**bit % 2)) * 2**bit
        return out

    barrier = pltpu.get_barrier_semaphore()
    for step in (1, NZ - 1):
        pl.semaphore_signal(
            barrier, inc=1, device_id={"head": (z + step) % NZ}, device_id_type=MESH
        )
    for m in range(1, 8):
        pl.semaphore_signal(barrier, inc=1, device_id={"ctx": flipped(m)}, device_id_type=MESH)

    for j in range(1, 4):
        pl.semaphore_signal(
            barrier,
            inc=1,
            device_id={"ctx": ((y_here + j) % 4 * 4 + x_here) * 2 + core},
            device_id_type=MESH,
        )
    c_copy = pltpu.make_async_copy(c_in, cotg.at[z], c_sem)
    c_copy.start()
    in_copies = [
        pltpu.make_async_copy(src, qkv.at[t], in_sem.at[t])
        for t, src in enumerate((q_in, k_in, v_in))
    ]
    for copy in in_copies:
        copy.start()
    w_copies = [
        pltpu.make_async_copy(w_in.at[:, pl.ds(j * WID, WID)], wb.at[j], w_sem.at[j])
        for j in range(NZ)
    ]
    for copy in w_copies:
        copy.start()

    pl.semaphore_wait(barrier, 2 + 7 + 3)

    def ag_region(d, block, chunk):
        return cotg.at[block, rows_of(chunk * HALF, HALF), :]

    def ag_chunk(d, i):
        return i % 2 if d == 0 else 1 - i % 2

    def ag_send(d, i):
        if d == 0:
            block, to = (z + NZ - i // 2) % NZ, (z + 1) % NZ
        else:
            block, to = (z + i // 2) % NZ, (z + NZ - 1) % NZ
        region = ag_region(d, block, ag_chunk(d, i))
        return pltpu.make_async_remote_copy(
            src_ref=region, dst_ref=region, send_sem=ag_s.at[d, i], recv_sem=ag_r.at[d, i],
            device_id={"head": to}, device_id_type=MESH,
        )

    def own_send(d, i):
        chunk = i if d == 0 else 1 - i
        return pltpu.make_async_remote_copy(
            src_ref=c_in.at[pl.ds(chunk * HALF, HALF), :], dst_ref=ag_region(d, z, chunk),
            send_sem=ag_s.at[d, i], recv_sem=ag_r.at[d, i],
            device_id={"head": (z + 1) % NZ if d == 0 else (z + NZ - 1) % NZ},
            device_id_type=MESH,
        )

    def ag_arrive(d, i):
        if d == 0:
            block = (z + 2 * NZ - 1 - i // 2) % NZ
        else:
            block = (z + 1 + i // 2) % NZ
        region = ag_region(d, block, ag_chunk(d, i))
        pltpu.make_async_remote_copy(
            src_ref=region, dst_ref=region, send_sem=ag_s.at[d, i], recv_sem=ag_r.at[d, i],
            device_id={"head": (z + 1) % NZ}, device_id_type=MESH,
        ).wait_recv()

    def ag_forward(i):
        for d in range(2):
            ag_arrive(d, i)
            ag_send(d, i + 2).start()

    for i in range(2):
        for d in range(2):
            own_send(d, i).start()
    c_copy.wait()

    row_id = lax.broadcasted_iota(jnp.int32, (BLK, BLK), 0)
    col_id = lax.broadcasted_iota(jnp.int32, (BLK, BLK), 1)
    perm[...] = jnp.where(col_id == row_id % 8 * 16 + row_id // 8, 1.0, 0.0).astype(BF)
    unperm[...] = jnp.where(row_id == col_id % 8 * 16 + col_id // 8, 1.0, 0.0).astype(BF)
    lmt[...] = jnp.full((8, DH), -3.0e38, F32)

    for t in (1, 2, 0):
        in_copies[t].wait()

        def pool(b, carry, t=t):
            x = dot(perm[...], qkv[t, rows_of(b * BLK, BLK), :])
            qkvp[t, rows_of(b * BLK, BLK), :] = x.astype(BF)
            one = halve(x.reshape(16, 8, WID))
            pool1[t, rows_of(b * 64, 64), :] = (one * 0.5).reshape(64, WID).astype(BF)
            two = halve(one)
            two_rows = (two * 0.25).reshape(32, WID).astype(BF)
            three = halve(two)
            three_rows = (three * 0.125).reshape(16, WID).astype(BF)
            if t == 0:
                qc2[rows_of(b * 32, 32), :] = two_rows
                qc3[rows_of(b * 16, 16), :] = three_rows
            else:
                kvs2[t - 1, rows_of(b * 32, 32), :] = two_rows
                kvs3[t - 1, rows_of(b * 16, 16), :] = three_rows
            p4[t, rows_of(b * 8, 8), :] = (halve(three) * 0.0625).reshape(8, WID)
            return carry

        lax.fori_loop(0, 4, pool, 0)
        if t == 0:
            qc4[...] = p4[0].astype(BF)
        else:
            kvs4[t - 1] = p4[t].astype(BF)

        if t == 2:
            kv_sends = []
            for m in range(1, 8):
                if m == 1:
                    src, dst, slot = kvs2, kvr.at[0], 0
                elif m < 4:
                    src, slot = kvs3, 1 + core
                    dst = kvr.at[1, :, rows_of(core * 64, 64), :]
                else:
                    src, slot = kvs4, 3 + c % 4
                    dst = kvr.at[2, :, rows_of(c % 4 * 32, 32), :]
                copy = pltpu.make_async_remote_copy(
                    src_ref=src, dst_ref=dst, send_sem=kv_s.at[m], recv_sem=kv_r.at[slot],
                    device_id={"ctx": flipped(m)}, device_id_type=MESH,
                )
                copy.start()
                kv_sends.append(copy)

    def kv_arrive():
        for slot in range(7):
            if slot == 0:
                src, dst = kvs2, kvr.at[0]
            elif slot < 3:
                src, dst = kvs3, kvr.at[1, :, pl.ds((slot - 1) * 64, 64), :]
            else:
                src, dst = kvs4, kvr.at[2, :, pl.ds((slot - 3) * 32, 32), :]
            pltpu.make_async_remote_copy(
                src_ref=src, dst_ref=dst, send_sem=kv_s.at[1], recv_sem=kv_r.at[slot],
                device_id={"ctx": flipped(1)}, device_id_type=MESH,
            ).wait_recv()

    tile_row = lax.broadcasted_iota(jnp.int32, (8, DH), 0)
    tile_col = lax.broadcasted_iota(jnp.int32, (8, DH), 1)

    def attend(h, level, start, count, queries, keys, values):
        scores = dot_nt(queries, keys) * SCALE
        peak = jnp.max(scores, axis=-1, keepdims=True)
        e = jnp.exp(scores - peak)
        total = jnp.sum(e, axis=-1, keepdims=True)
        wide = jnp.broadcast_to(peak, (count, DH))
        at = pl.ds(start, count) if isinstance(start, int) else start
        pk[h, at, :] = wide + level * LOG_TWO
        tt[h, at, :] = jnp.broadcast_to(total, (count, DH))
        nm[h, at, :] = dot(e.astype(BF), values)
        top = jnp.max(wide.reshape(count // 8, 8, DH), axis=0)
        top = jnp.broadcast_to(jnp.max(top, axis=0, keepdims=True), (8, DH))
        here = jnp.logical_and(tile_row == h, tile_col == level)
        lmt[...] = jnp.where(here, jnp.maximum(lmt[...], top), lmt[...])
        return e

    def lanes(h):
        return rows_of(h * DH, DH)

    def near_forward(h, carry):
        hs = lanes(h)
        for p in range(2):
            at = pl.ds(p * 256, 256)
            e0[h, p] = attend(h, 0, p * 256, 256, qkvp[0, at, hs], qkvp[1, at, hs], qkvp[2, at, hs])
        for g in range(2):
            other = pl.ds((1 - g) * 128, 128)
            e1[h, g] = attend(
                h, 1, OFF[1] + g * 128, 128,
                pool1[0, pl.ds(g * 128, 128), hs], pool1[1, other, hs], pool1[2, other, hs],
            )
        return carry

    lax.fori_loop(0, HEADS, near_forward, 0)
    ag_forward(0)
    ag_forward(1)
    kv_arrive()

    def far_forward(h, carry):
        hs = lanes(h)
        for level, queries, store in ((2, qc2, e2), (3, qc3, e3), (4, qc4, e4)):
            count = TOK >> level
            store[h] = attend(
                h, level, OFF[level], count,
                queries[:, hs], kvr[level - 2, 0, :, hs], kvr[level - 2, 1, :, hs],
            )

        def merge(b, inner):
            def level_rows(ref, level):
                n = BLK >> level
                return expand(ref[h, rows_of(OFF[level] + b * n, n), :].reshape(n // 8, 8, DH), 16)

            peaks = [level_rows(pk, level) for level in range(LEVELS)]
            highest = peaks[0]
            for other in peaks[1:]:
                highest = jnp.maximum(highest, other)
            scales = [jnp.exp(peak - highest) for peak in peaks]
            den = scales[0] * level_rows(tt, 0)
            num = scales[0] * level_rows(nm, 0)
            for level in range(1, LEVELS):
                den = den + scales[level] * level_rows(tt, level)
                num = num + scales[level] * level_rows(nm, level)
            inv = 1.0 / den
            at = rows_of(b * BLK, BLK)
            for level in range(LEVELS):
                wts5[h, level, at, :] = (scales[level] * inv).reshape(BLK, DH)
            out = (num * inv).reshape(BLK, DH)
            af[h, at, :] = out
            ap[at, hs] = out.astype(BF)
            return inner

        lax.fori_loop(0, 4, merge, 0)
        return carry

    lax.fori_loop(0, HEADS, far_forward, 0)
    ag_forward(2)

    lmsib_copy = pltpu.make_async_remote_copy(
        src_ref=lmt, dst_ref=lmsib, send_sem=lmsib_s, recv_sem=lmsib_r,
        device_id={"ctx": flipped(1)}, device_id_type=MESH,
    )
    lmsib_copy.start()

    def restore(b, carry):
        at = rows_of(b * BLK, BLK)
        attn[at, :] = dot(unperm[...], ap[at, :]).astype(BF)
        return carry

    lax.fori_loop(0, 4, restore, 0)

    def turn(f, carry):
        attnt[rows_of(f * DH, DH), :] = attn[:, rows_of(f * DH, DH)].astype(F32).T.astype(BF)
        return carry

    lax.fori_loop(0, HEADS, turn, 0)
    for copy in w_copies:
        copy.wait()

    def sib_copy(block):
        return pltpu.make_async_remote_copy(
            src_ref=sibs.at[block], dst_ref=sibr.at[block],
            send_sem=sib_s.at[block], recv_sem=sib_r.at[block],
            device_id={"ctx": flipped(1)}, device_id_type=MESH,
        )

    def x_copy(owner, sender):
        return pltpu.make_async_remote_copy(
            src_ref=wsend.at[owner], dst_ref=wrecv.at[owner // 4, sender],
            send_sem=w_s.at[owner], recv_sem=w_r.at[owner // 4, sender],
            device_id={"ctx": (y_here * 4 + owner % 4) * 2 + core}, device_id_type=MESH,
        )

    def y_copy(to_y, sender):
        return pltpu.make_async_remote_copy(
            src_ref=ysend.at[to_y], dst_ref=yrecv.at[sender],
            send_sem=y_s.at[to_y], recv_sem=y_r.at[sender],
            device_id={"ctx": (to_y * 4 + x_here) * 2 + core}, device_id_type=MESH,
        )

    def block_terms(block, slot, first=False):
        def part(r, carry):
            at = rows_of(r * HALF, HALF)
            term = dot_nt(cotg[block, at, :], wb[block])
            gacc[at, :] = term if first else gacc[at, :] + term
            weight = dot(attnt[at, :], cotg[block])
            for m in range(4):
                wtile[m] = weight[:, m * DH : (m + 1) * DH]
            for i in range(2):
                wown[slot, i, at, :] = wtile[2 * i + core]
                sibs[block, i, at, :] = wtile[2 * i + 1 - core].astype(BF)
            return carry

        lax.fori_loop(0, 2, part, 0)
        sib_copy(block).start()

    def block_share(block, slot):
        sib_copy(block).wait_recv()
        for i in range(2):
            owner = 2 * block + i
            total = wown[slot, i] + sibr[block, i].astype(F32)

            @pl.when(owner % 4 == x_here)
            def _():
                wrow[owner // 4] = total

            @pl.when(owner % 4 != x_here)
            def _():
                wsend[owner] = total.astype(BF)
                x_copy(owner, x_here).start()

    def row_share(block):
        to_y = block // 2

        @pl.when(block % 2 == x_here // 2)
        def _():
            for j in range(1, 4):
                sender = (x_here + j) % 4
                x_copy(to_y * 4 + x_here, sender).wait_recv()
            total = wrow[to_y]
            for j in range(1, 4):
                total = total + wrecv[to_y, (x_here + j) % 4].astype(F32)

            @pl.when(to_y == y_here)
            def _():
                wmine[...] = total

            @pl.when(to_y != y_here)
            def _():
                ysend[to_y] = total.astype(BF)
                y_copy(to_y, y_here).start()

    def nth_block(n):
        return (z + NZ + (1 - 2 * (n % 2)) * ((n + 1) // 2)) % NZ

    def blocks(first, last):
        def one(n, carry):
            block_terms(nth_block(n), n % 2)
            block_share(nth_block(n - 1), (n - 1) % 2)
            return carry

        lax.fori_loop(first, last, one, 0)

    block_terms(z, 0, first=True)
    ag_forward(3)
    blocks(1, 3)
    ag_forward(4)

    def mixed_part(block, chunk):
        return dot(attn[rows_of(chunk * HALF, HALF), :], wb[block])

    def rs_copy(d, i):
        return pltpu.make_async_remote_copy(
            src_ref=rss.at[d, i], dst_ref=rsr.at[d, i],
            send_sem=rs_s.at[d, i], recv_sem=rs_r.at[d, i],
            device_id={"head": (z + 1) % NZ if d == 0 else (z + NZ - 1) % NZ},
            device_id_type=MESH,
        )

    def rs_part(d, i):
        distance = 4 - (i + 1) // 2
        block = (z + distance) % NZ if d == 0 else (z + NZ - distance) % NZ
        return mixed_part(block, ag_chunk(d, i))

    def rs_relay(i):
        for d in range(2):
            held[d] = rs_part(d, i + 2)
        for d in range(2):
            rs_copy(d, i).wait_recv()
            rss[d, i + 2] = (held[d] + rsr[d, i].astype(F32)).astype(BF)
            rs_copy(d, i + 2).start()

    for i in range(2):
        for d in range(2):
            rss[d, i] = rs_part(d, i).astype(BF)
            rs_copy(d, i).start()

    lmsib_copy.wait()
    lm2[0] = jnp.maximum(lmt[...], lmsib[...])

    def lm_copy(stage, to, slot):
        chip_to = y_here * 4 + to if stage == 0 else to * 4 + x_here
        return pltpu.make_async_remote_copy(
            src_ref=lm2.at[stage], dst_ref=lmr.at[stage, slot],
            send_sem=lm_s.at[stage, to], recv_sem=lm_r.at[stage, slot],
            device_id={"ctx": chip_to * 2 + core}, device_id_type=MESH,
        )

    places = (x_here, y_here)

    def lm_start(stage):
        for j in range(1, 4):
            lm_copy(stage, (places[stage] + j) % 4, places[stage]).start()

    def lm_gather(stage):
        total = lm2[stage]
        for j in range(1, 4):
            slot = (places[stage] + j) % 4
            lm_copy(stage, slot, slot).wait_recv()
            total = jnp.maximum(total, lmr[stage, slot])
        return total

    lm_start(0)

    blocks(3, 5)
    for d in range(2):
        ag_arrive(d, 5)
    blocks(5, 7)
    for d in range(2):
        ag_arrive(d, 6)
    blocks(7, 8)

    def permute_grad(b, carry):
        at = rows_of(b * BLK, BLK)
        gp[at, :] = dot(perm[...], gacc[at, :].astype(BF)).astype(BF)
        return carry

    lax.fori_loop(0, 4, permute_grad, 0)
    block_share(nth_block(7), 1)

    rsc, dq, rg = pk, tt, nm

    def score_grads(h, level, at, e, queries, keys, values):
        grad = rg[h, at, :].astype(BF)
        weights = dot_nt(grad, values)
        dz = (e * (weights - rsc[h, at, :][:, :1])).astype(BF)
        dq[h, at, :] = dot(dz, keys) * (SCALE * 0.5**level)
        return dot_tn(dz, queries) * SCALE, dot_tn(e.astype(BF), grad)

    def far_backward(h, carry):
        hs = lanes(h)

        def spread(b, inner):
            at = rows_of(b * BLK, BLK)
            g = gp[at, hs].astype(F32)
            delta = jnp.sum(g * af[h, at, :], axis=-1, keepdims=True)
            g = g.reshape(16, 8, DH)
            delta = jnp.broadcast_to(delta, (BLK, DH)).reshape(16, 8, DH)
            for level in range(LEVELS):
                share = wts5[h, level, at, :].reshape(16, 8, DH)
                grads, scalars = share * g, share * delta
                for _ in range(level):
                    grads, scalars = halve(grads), halve(scalars)
                n = BLK >> level
                put = rows_of(OFF[level] + b * n, n)
                rg[h, put, :] = grads.reshape(n, DH)
                rsc[h, put, :] = scalars.reshape(n, DH)
            return inner

        lax.fori_loop(0, 4, spread, 0)
        for level, queries, store in ((2, qc2, e2), (3, qc3, e3), (4, qc4, e4)):
            dk, dv = score_grads(
                h, level, pl.ds(OFF[level], TOK >> level), store[h],
                queries[:, hs], kvr[level - 2, 0, :, hs], kvr[level - 2, 1, :, hs],
            )
            gks[level - 2, 0, :, hs] = (dk * 0.5**level).astype(BF)
            gks[level - 2, 1, :, hs] = (dv * 0.5**level).astype(BF)
        return carry

    lax.fori_loop(0, 2, far_backward, 0)
    rs_relay(0)
    lax.fori_loop(2, HEADS, far_backward, 0)

    gk_sends = []
    for m in range(1, 8):
        if m == 1:
            src, dst, slot = gks.at[0], gkr2, 0
        elif m < 4:
            src = gks.at[1, :, rows_of(flipped(m) % 2 * 64, 64), :]
            dst, slot = gkr3.at[core], 1 + core
        else:
            src = gks.at[2, :, rows_of(flipped(m) % 4 * 32, 32), :]
            dst, slot = gkr4.at[c % 4], 3 + c % 4
        copy = pltpu.make_async_remote_copy(
            src_ref=src, dst_ref=dst, send_sem=gk_s.at[m], recv_sem=gk_r.at[slot],
            device_id={"ctx": flipped(m)}, device_id_type=MESH,
        )
        copy.start()
        gk_sends.append(copy)

    def near_backward(h, carry):
        hs = lanes(h)
        for p in range(2):
            at = pl.ds(p * 256, 256)
            dk, dv = score_grads(
                h, 0, at, e0[h, p], qkvp[0, at, hs], qkvp[1, at, hs], qkvp[2, at, hs]
            )
            gkp[at, hs] = dk
            gvp[at, hs] = dv
        for g in range(2):
            other = pl.ds((1 - g) * 128, 128)
            dk, dv = score_grads(
                h, 1, pl.ds(OFF[1] + g * 128, 128), e1[h, g],
                pool1[0, pl.ds(g * 128, 128), hs], pool1[1, other, hs], pool1[2, other, hs],
            )
            to = pl.ds((1 - g) * 256, 256)
            for ref, part in ((gkp, dk), (gvp, dv)):
                wide = expand((part * 0.5).reshape(16, 8, DH), 32).reshape(256, DH)
                ref[to, hs] = ref[to, hs] + wide

        def gather_q(b, inner):
            total = dq[h, rows_of(b * BLK, BLK), :].reshape(16, 8, DH)
            for level in range(1, LEVELS):
                n = BLK >> level
                part = dq[h, rows_of(OFF[level] + b * n, n), :].reshape(n // 8, 8, DH)
                total = total + expand(part, 16)
            gqp[rows_of(b * BLK, BLK), hs] = total.reshape(BLK, DH)
            return inner

        lax.fori_loop(0, 4, gather_q, 0)
        return carry

    def row_shares(first, last):
        def one(n, carry):
            row_share(nth_block(n))
            return carry

        lax.fori_loop(first, last, one, 0)

    lax.fori_loop(0, 2, near_backward, 0)
    rs_relay(1)
    row_shares(0, 3)
    lm2[1] = lm_gather(0)
    lm_start(1)
    lax.fori_loop(2, HEADS, near_backward, 0)
    rs_relay(2)
    row_shares(3, 7)

    def token_order(ref, b):
        at = rows_of(b * BLK, BLK)
        x = ref[at, :]
        high = x.astype(BF)
        low = (x - high.astype(F32)).astype(BF)
        ref[at, :] = dot(unperm[...], high) + dot(unperm[...], low)

    def finish_q(b, carry):
        token_order(gqp, b)
        return carry

    lax.fori_loop(0, 4, finish_q, 0)
    mix[pl.ds(0, HALF), :] = mixed_part(z, 0)
    mix[pl.ds(HALF, HALF), :] = mixed_part(z, 1)
    rs_relay(3)
    row_shares(7, 8)

    for slot in range(7):
        if slot == 0:
            src, dst = gks.at[0], gkr2
        elif slot < 3:
            src, dst = gks.at[1, :, pl.ds(0, 64), :], gkr3.at[slot - 1]
        else:
            src, dst = gks.at[2, :, pl.ds(0, 32), :], gkr4.at[slot - 3]
        pltpu.make_async_remote_copy(
            src_ref=src, dst_ref=dst, send_sem=gk_s.at[1], recv_sem=gk_r.at[slot],
            device_id={"ctx": flipped(1)}, device_id_type=MESH,
        ).wait_recv()

    for t, own in enumerate((gkp, gvp)):
        p4[t] = sum(gkr4[s, t].astype(F32) for s in range(4))

        def finish_kv(b, carry, t=t, own=own):
            at = rows_of(b * BLK, BLK)
            two = gkr2[t, rows_of(b * 32, 32), :].astype(F32)
            three = gkr3[0, t, rows_of(b * 16, 16), :].astype(F32)
            three = three + gkr3[1, t, rows_of(b * 16, 16), :].astype(F32)
            four = p4[t, rows_of(b * 8, 8), :]
            low = expand(three.reshape(2, 8, WID), 4) + expand(four.reshape(1, 8, WID), 4)
            low = low + two.reshape(4, 8, WID)
            own[at, :] = own[at, :] + expand(low, 16).reshape(BLK, WID)
            token_order(own, b)
            return carry

        lax.fori_loop(0, 4, finish_kv, 0)

    rs_relay(4)

    for j in range(1, 4):
        y_copy(y_here, (y_here + j) % 4).wait_recv()
    total = wmine[...]
    for j in range(1, 4):
        total = total + yrecv[(y_here + j) % 4].astype(F32)
    wmine[...] = total

    lm_out[...] = lm_gather(1)[:HEADS, :LEVELS]

    for i, chunks in ((5, (1, 0)), (6, (0, 1))):
        for d in range(2):
            rs_copy(d, i).wait_recv()
            at = pl.ds(chunks[d] * HALF, HALF)
            mix[at, :] = mix[at, :] + rsr[d, i].astype(F32)

    for copy in kv_sends + gk_sends:
        copy.wait_send()

    def drain(i, carry):
        for d in range(2):
            ag_send(d, i).wait_send()
            rs_copy(d, i).wait_send()
        return carry

    lax.fori_loop(0, 7, drain, 0)

    def drain_sib(i, carry):
        sib_copy(i).wait_send()
        return carry

    lax.fori_loop(0, NZ, drain_sib, 0)

    def drain_chips(j, carry):
        to = (chip + j) % CHIPS

        @pl.when(to % 4 != x_here)
        def _():
            x_copy(to, x_here).wait_send()

        return carry

    lax.fori_loop(1, CHIPS, drain_chips, 0)
    for j in range(1, 4):
        y_copy((y_here + j) % 4, y_here).wait_send()
        for stage in range(2):
            lm_copy(stage, (places[stage] + j) % 4, places[stage]).wait_send()


def finish(*refs):
    sems = refs[-1]
    copies = []
    for t in range(6):
        pieces = 2 if t == 0 else 1
        size = refs[t].shape[0] // pieces
        for piece in range(pieces):
            at = pl.ds(piece * size, size)
            copies.append(
                pltpu.make_async_copy(
                    refs[t].at[at, :], refs[6 + t].at[at, :], sems.at[len(copies)]
                )
            )
    for copy in copies:
        copy.start()
    for copy in copies:
        copy.wait()


def vmem(shape, kind):
    return pltpu.VMEM(shape, kind)


def per_device(query_input, key_input, value_input, out_weight, out_cotangent):
    dma = pltpu.SemaphoreType.DMA
    scratch = [
        vmem((3, TOK, WID), BF),
        vmem((BLK, BLK), BF),
        vmem((BLK, BLK), BF),
        vmem((3, TOK, WID), BF),
        vmem((3, 256, WID), BF),
        vmem((128, WID), BF),
        vmem((64, WID), BF),
        vmem((3, 32, WID), F32),
        vmem((32, WID), BF),
        vmem((2, 128, WID), BF),
        vmem((2, 64, WID), BF),
        vmem((2, 32, WID), BF),
        vmem((3, 2, 128, WID), BF),
        vmem((HEADS, 2, 256, 256), F32),
        vmem((HEADS, 2, 128, 128), F32),
        vmem((HEADS, 128, 128), F32),
        vmem((HEADS, 64, 128), F32),
        vmem((HEADS, 32, 128), F32),
        vmem((HEADS, ROWS, DH), F32),
        vmem((HEADS, ROWS, DH), F32),
        vmem((HEADS, ROWS, DH), F32),
        vmem((HEADS, LEVELS, TOK, DH), F32),
        vmem((HEADS, TOK, DH), F32),
        vmem((TOK, WID), BF),
        vmem((TOK, WID), BF),
        vmem((WID, TOK), BF),
        vmem((NZ, TOK, WID), BF),
        vmem((NZ, WID, WID), BF),
        vmem((TOK, WID), F32),
        vmem((TOK, WID), BF),
        vmem((4, HALF, DH), F32),
        vmem((2, 2, WID, DH), F32),
        vmem((NZ, 2, WID, DH), BF),
        vmem((NZ, 2, WID, DH), BF),
        vmem((CHIPS, WID, DH), BF),
        vmem((4, 4, WID, DH), BF),
        vmem((4, WID, DH), F32),
        vmem((4, WID, DH), BF),
        vmem((4, WID, DH), BF),
        vmem((2, 7, HALF, WID), BF),
        vmem((2, 7, HALF, WID), BF),
        vmem((2, HALF, WID), F32),
        vmem((3, 2, 128, WID), BF),
        vmem((2, 128, WID), BF),
        vmem((2, 2, 64, WID), BF),
        vmem((4, 2, 32, WID), BF),
        vmem((8, DH), F32),
        vmem((8, DH), F32),
        vmem((2, 8, DH), F32),
        vmem((2, 4, 8, DH), F32),
        dma((3,)), dma((NZ,)), dma,
        dma((2, 7)), dma((2, 7)),
        dma((8,)), dma((7,)), dma((8,)), dma((7,)),
        dma((NZ,)), dma((NZ,)), dma((CHIPS,)), dma((4, 4)), dma((4,)), dma((4,)),
        dma((2, 7)), dma((2, 7)),
        dma, dma, dma((2, 4)), dma((2, 4)),
    ]
    outs = pl.pallas_call(
        kernel,
        out_shape=tuple(vmem((TOK, WID), F32) for _ in range(4))
        + (vmem((WID, DH), F32), vmem((HEADS, LEVELS), F32)),
        in_specs=[pl.BlockSpec(memory_space=pl.ANY)] * 5,
        out_specs=[pl.BlockSpec(memory_space=pltpu.VMEM)] * 6,
        scratch_shapes=scratch,
        compiler_params=pltpu.CompilerParams(
            collective_id=0, has_side_effects=True, vmem_limit_bytes=56000000
        ),
        name="layer",
    )(query_input, key_input, value_input, out_weight, out_cotangent)
    held = [pltpu.with_memory_space_constraint(x, pltpu.VMEM) for x in outs]
    anywhere = pl.BlockSpec(memory_space=pl.ANY)
    local = pl.BlockSpec(memory_space=pltpu.VMEM)
    wide = jax.ShapeDtypeStruct((TOK, WID), F32)
    outs = pl.pallas_call(
        finish,
        out_shape=(
            wide, wide, wide, wide,
            jax.ShapeDtypeStruct((WID, DH), F32),
            jax.ShapeDtypeStruct((HEADS, LEVELS), F32),
        ),
        in_specs=[local] * 6,
        out_specs=[anywhere] * 6,
        scratch_shapes=[dma((18,))],
        compiler_params=pltpu.CompilerParams(vmem_limit_bytes=1000000),
        name="finish",
    )(*held)
    return outs[:5] + (outs[5].T,)


def solution(mesh):
    in_specs = (
        P("ctx", "head"),
        P("ctx", "head"),
        P("ctx", "head"),
        P("head", None),
        P("ctx", "head"),
    )
    out_specs = (
        P("ctx", "head"),
        P("ctx", "head"),
        P("ctx", "head"),
        P("ctx", "head"),
        P("head", "ctx"),
        P(None, "head"),
    )
    return jax.shard_map(
        per_device, mesh=mesh, in_specs=in_specs, out_specs=out_specs, check_vma=False
    )
```

```python
import functools
import math

import jax
import jax.numpy as jnp
from jax import lax
from jax.experimental import pallas as pl
from jax.experimental.pallas import tpu as pltpu
from jax.sharding import PartitionSpec as P

DH = 128
BLK = 128
LEVELS = 5
NZ = 8
NCTX = 32
CHIPS = 16
HEADS = 4
TOK = 512
WID = HEADS * DH
HALF = TOK // 2
LOG_TWO = math.log(2.0)
SCALE = DH ** (-0.5)
MESH = pl.DeviceIdType.MESH
BF = jnp.bfloat16
F32 = jnp.float32
OFF = (0, 512, 768, 896, 960)
ROWS = 992


def dot(a, b):
    return lax.dot_general(a, b, (((1,), (0,)), ((), ())), preferred_element_type=F32)


def dot_nt(a, b):
    return lax.dot_general(a, b, (((1,), (1,)), ((), ())), preferred_element_type=F32)


def dot_tn(a, b):
    return lax.dot_general(a, b, (((0,), (0,)), ((), ())), preferred_element_type=F32)


def rows_of(start, size):
    return pl.ds(pl.multiple_of(start, size), size)


def expand(x, slabs):
    n = x.shape[0]
    if n == slabs:
        return x
    return jnp.broadcast_to(x[:, None], (n, slabs // n, 8, x.shape[2])).reshape(
        slabs, 8, x.shape[2]
    )


def halve(x):
    y = x.reshape(x.shape[0] // 2, 2, 8, x.shape[2])
    return y[:, 0] + y[:, 1]


def kernel(
    q_in, k_in, v_in, w_in, c_in,
    mix, gqp, gkp, gvp, wmine, lm_out,
    qkv, perm, unperm, qkvp, pool1, qc2, qc3, p4, qc4, kvs2, kvs3, kvs4, kvr,
    e0, e1, e2, e3, e4, pk, tt, nm, wts5, af, ap, attn, attnt,
    cotg, wb, gacc, gp, wtile, wown, sibs, sibr, wsend, wrecv, wrow, ysend, yrecv,
    rss, rsr, held, gks, gkr2, gkr3, gkr4, lmt, lmsib, lm2, lmr,
    in_sem, w_sem, c_sem, ag_s, ag_r, kv_s, kv_r, gk_s, gk_r,
    sib_s, sib_r, w_s, w_r, y_s, y_r, rs_s, rs_r, lmsib_s, lmsib_r, lm_s, lm_r,
):
    c = lax.axis_index("ctx")
    z = lax.axis_index("head")
    core = c % 2
    chip = c // 2
    x_here, y_here = chip % 4, chip // 4

    def flipped(m):
        out = c
        for bit in range(3):
            if m >> bit & 1:
                out = out + (1 - 2 * (c // 2**bit % 2)) * 2**bit
        return out

    barrier = pltpu.get_barrier_semaphore()
    for step in (1, NZ - 1):
        pl.semaphore_signal(
            barrier, inc=1, device_id={"head": (z + step) % NZ}, device_id_type=MESH
        )
    for m in range(1, 8):
        pl.semaphore_signal(barrier, inc=1, device_id={"ctx": flipped(m)}, device_id_type=MESH)

    for j in range(1, 4):
        pl.semaphore_signal(
            barrier,
            inc=1,
            device_id={"ctx": ((y_here + j) % 4 * 4 + x_here) * 2 + core},
            device_id_type=MESH,
        )
    c_copy = pltpu.make_async_copy(c_in, cotg.at[z], c_sem)
    c_copy.start()
    in_copies = [
        pltpu.make_async_copy(src, qkv.at[t], in_sem.at[t])
        for t, src in enumerate((q_in, k_in, v_in))
    ]
    for copy in in_copies:
        copy.start()
    w_copies = [
        pltpu.make_async_copy(w_in.at[:, pl.ds(j * WID, WID)], wb.at[j], w_sem.at[j])
        for j in range(NZ)
    ]
    for copy in w_copies:
        copy.start()

    pl.semaphore_wait(barrier, 2 + 7 + 3)

    def ag_region(d, block, chunk):
        return cotg.at[block, rows_of(chunk * HALF, HALF), :]

    def ag_chunk(d, i):
        return i % 2 if d == 0 else 1 - i % 2

    def ag_send(d, i):
        if d == 0:
            block, to = (z + NZ - i // 2) % NZ, (z + 1) % NZ
        else:
            block, to = (z + i // 2) % NZ, (z + NZ - 1) % NZ
        region = ag_region(d, block, ag_chunk(d, i))
        return pltpu.make_async_remote_copy(
            src_ref=region, dst_ref=region, send_sem=ag_s.at[d, i], recv_sem=ag_r.at[d, i],
            device_id={"head": to}, device_id_type=MESH,
        )

    def own_send(d, i):
        chunk = i if d == 0 else 1 - i
        return pltpu.make_async_remote_copy(
            src_ref=c_in.at[pl.ds(chunk * HALF, HALF), :], dst_ref=ag_region(d, z, chunk),
            send_sem=ag_s.at[d, i], recv_sem=ag_r.at[d, i],
            device_id={"head": (z + 1) % NZ if d == 0 else (z + NZ - 1) % NZ},
            device_id_type=MESH,
        )

    def ag_arrive(d, i):
        if d == 0:
            block = (z + 2 * NZ - 1 - i // 2) % NZ
        else:
            block = (z + 1 + i // 2) % NZ
        region = ag_region(d, block, ag_chunk(d, i))
        pltpu.make_async_remote_copy(
            src_ref=region, dst_ref=region, send_sem=ag_s.at[d, i], recv_sem=ag_r.at[d, i],
            device_id={"head": (z + 1) % NZ}, device_id_type=MESH,
        ).wait_recv()

    def ag_forward(i):
        for d in range(2):
            ag_arrive(d, i)
            ag_send(d, i + 2).start()

    for i in range(2):
        for d in range(2):
            own_send(d, i).start()
    c_copy.wait()

    row_id = lax.broadcasted_iota(jnp.int32, (BLK, BLK), 0)
    col_id = lax.broadcasted_iota(jnp.int32, (BLK, BLK), 1)
    perm[...] = jnp.where(col_id == row_id % 8 * 16 + row_id // 8, 1.0, 0.0).astype(BF)
    unperm[...] = jnp.where(row_id == col_id % 8 * 16 + col_id // 8, 1.0, 0.0).astype(BF)
    lmt[...] = jnp.full((8, DH), -3.0e38, F32)

    for t in (1, 2, 0):
        in_copies[t].wait()

        def pool(b, carry, t=t):
            x = dot(perm[...], qkv[t, rows_of(b * BLK, BLK), :])
            qkvp[t, rows_of(b * BLK, BLK), :] = x.astype(BF)
            one = halve(x.reshape(16, 8, WID))
            pool1[t, rows_of(b * 64, 64), :] = (one * 0.5).reshape(64, WID).astype(BF)
            two = halve(one)
            two_rows = (two * 0.25).reshape(32, WID).astype(BF)
            three = halve(two)
            three_rows = (three * 0.125).reshape(16, WID).astype(BF)
            if t == 0:
                qc2[rows_of(b * 32, 32), :] = two_rows
                qc3[rows_of(b * 16, 16), :] = three_rows
            else:
                kvs2[t - 1, rows_of(b * 32, 32), :] = two_rows
                kvs3[t - 1, rows_of(b * 16, 16), :] = three_rows
            p4[t, rows_of(b * 8, 8), :] = (halve(three) * 0.0625).reshape(8, WID)
            return carry

        lax.fori_loop(0, 4, pool, 0)
        if t == 0:
            qc4[...] = p4[0].astype(BF)
        else:
            kvs4[t - 1] = p4[t].astype(BF)

        if t == 2:
            kv_sends = []
            for m in range(1, 8):
                if m == 1:
                    src, dst, slot = kvs2, kvr.at[0], 0
                elif m < 4:
                    src, slot = kvs3, 1 + core
                    dst = kvr.at[1, :, rows_of(core * 64, 64), :]
                else:
                    src, slot = kvs4, 3 + c % 4
                    dst = kvr.at[2, :, rows_of(c % 4 * 32, 32), :]
                copy = pltpu.make_async_remote_copy(
                    src_ref=src, dst_ref=dst, send_sem=kv_s.at[m], recv_sem=kv_r.at[slot],
                    device_id={"ctx": flipped(m)}, device_id_type=MESH,
                )
                copy.start()
                kv_sends.append(copy)

    def kv_arrive():
        for slot in range(7):
            if slot == 0:
                src, dst = kvs2, kvr.at[0]
            elif slot < 3:
                src, dst = kvs3, kvr.at[1, :, pl.ds((slot - 1) * 64, 64), :]
            else:
                src, dst = kvs4, kvr.at[2, :, pl.ds((slot - 3) * 32, 32), :]
            pltpu.make_async_remote_copy(
                src_ref=src, dst_ref=dst, send_sem=kv_s.at[1], recv_sem=kv_r.at[slot],
                device_id={"ctx": flipped(1)}, device_id_type=MESH,
            ).wait_recv()

    tile_row = lax.broadcasted_iota(jnp.int32, (8, DH), 0)
    tile_col = lax.broadcasted_iota(jnp.int32, (8, DH), 1)

    def attend(h, level, start, count, queries, keys, values):
        scores = dot_nt(queries, keys) * SCALE
        peak = jnp.max(scores, axis=-1, keepdims=True)
        e = jnp.exp(scores - peak)
        total = jnp.sum(e, axis=-1, keepdims=True)
        wide = jnp.broadcast_to(peak, (count, DH))
        at = pl.ds(start, count) if isinstance(start, int) else start
        pk[h, at, :] = wide + level * LOG_TWO
        tt[h, at, :] = jnp.broadcast_to(total, (count, DH))
        nm[h, at, :] = dot(e.astype(BF), values)
        top = jnp.max(wide.reshape(count // 8, 8, DH), axis=0)
        top = jnp.broadcast_to(jnp.max(top, axis=0, keepdims=True), (8, DH))
        here = jnp.logical_and(tile_row == h, tile_col == level)
        lmt[...] = jnp.where(here, jnp.maximum(lmt[...], top), lmt[...])
        return e

    def lanes(h):
        return rows_of(h * DH, DH)

    def near_forward(h, carry):
        hs = lanes(h)
        for p in range(2):
            at = pl.ds(p * 256, 256)
            e0[h, p] = attend(h, 0, p * 256, 256, qkvp[0, at, hs], qkvp[1, at, hs], qkvp[2, at, hs])
        for g in range(2):
            other = pl.ds((1 - g) * 128, 128)
            e1[h, g] = attend(
                h, 1, OFF[1] + g * 128, 128,
                pool1[0, pl.ds(g * 128, 128), hs], pool1[1, other, hs], pool1[2, other, hs],
            )
        return carry

    lax.fori_loop(0, 2, near_forward, 0)
    ag_forward(0)
    lax.fori_loop(2, HEADS, near_forward, 0)
    ag_forward(1)
    kv_arrive()

    def far_forward(h, carry):
        hs = lanes(h)
        for level, queries, store in ((2, qc2, e2), (3, qc3, e3), (4, qc4, e4)):
            count = TOK >> level
            store[h] = attend(
                h, level, OFF[level], count,
                queries[:, hs], kvr[level - 2, 0, :, hs], kvr[level - 2, 1, :, hs],
            )

        def merge(b, inner):
            def level_rows(ref, level):
                n = BLK >> level
                return expand(ref[h, rows_of(OFF[level] + b * n, n), :].reshape(n // 8, 8, DH), 16)

            peaks = [level_rows(pk, level) for level in range(LEVELS)]
            highest = peaks[0]
            for other in peaks[1:]:
                highest = jnp.maximum(highest, other)
            scales = [jnp.exp(peak - highest) for peak in peaks]
            den = scales[0] * level_rows(tt, 0)
            num = scales[0] * level_rows(nm, 0)
            for level in range(1, LEVELS):
                den = den + scales[level] * level_rows(tt, level)
                num = num + scales[level] * level_rows(nm, level)
            inv = 1.0 / den
            at = rows_of(b * BLK, BLK)
            for level in range(LEVELS):
                wts5[h, level, at, :] = (scales[level] * inv).reshape(BLK, DH)
            out = (num * inv).reshape(BLK, DH)
            af[h, at, :] = out
            ap[at, hs] = out.astype(BF)
            return inner

        lax.fori_loop(0, 4, merge, 0)
        return carry

    lax.fori_loop(0, HEADS, far_forward, 0)
    ag_forward(2)

    lmsib_copy = pltpu.make_async_remote_copy(
        src_ref=lmt, dst_ref=lmsib, send_sem=lmsib_s, recv_sem=lmsib_r,
        device_id={"ctx": flipped(1)}, device_id_type=MESH,
    )
    lmsib_copy.start()

    def restore(b, carry):
        at = rows_of(b * BLK, BLK)
        attn[at, :] = dot(unperm[...], ap[at, :]).astype(BF)
        return carry

    lax.fori_loop(0, 4, restore, 0)

    def turn(f, carry):
        attnt[rows_of(f * DH, DH), :] = attn[:, rows_of(f * DH, DH)].astype(F32).T.astype(BF)
        return carry

    lax.fori_loop(0, HEADS, turn, 0)
    for copy in w_copies:
        copy.wait()

    def sib_copy(block):
        return pltpu.make_async_remote_copy(
            src_ref=sibs.at[block], dst_ref=sibr.at[block],
            send_sem=sib_s.at[block], recv_sem=sib_r.at[block],
            device_id={"ctx": flipped(1)}, device_id_type=MESH,
        )

    def x_copy(owner, sender):
        return pltpu.make_async_remote_copy(
            src_ref=wsend.at[owner], dst_ref=wrecv.at[owner // 4, sender],
            send_sem=w_s.at[owner], recv_sem=w_r.at[owner // 4, sender],
            device_id={"ctx": (y_here * 4 + owner % 4) * 2 + core}, device_id_type=MESH,
        )

    def y_copy(to_y, sender):
        return pltpu.make_async_remote_copy(
            src_ref=ysend.at[to_y], dst_ref=yrecv.at[sender],
            send_sem=y_s.at[to_y], recv_sem=y_r.at[sender],
            device_id={"ctx": (to_y * 4 + x_here) * 2 + core}, device_id_type=MESH,
        )

    def block_terms(block, slot, first=False):
        def part(r, carry):
            at = rows_of(r * HALF, HALF)
            term = dot_nt(cotg[block, at, :], wb[block])
            gacc[at, :] = term if first else gacc[at, :] + term
            weight = dot(attnt[at, :], cotg[block])
            for m in range(4):
                wtile[m] = weight[:, m * DH : (m + 1) * DH]
            for i in range(2):
                wown[slot, i, at, :] = wtile[2 * i + core]
                sibs[block, i, at, :] = wtile[2 * i + 1 - core].astype(BF)
            return carry

        lax.fori_loop(0, 2, part, 0)
        sib_copy(block).start()

    def block_share(block, slot):
        sib_copy(block).wait_recv()
        for i in range(2):
            owner = 2 * block + i
            total = wown[slot, i] + sibr[block, i].astype(F32)

            @pl.when(owner % 4 == x_here)
            def _():
                wrow[owner // 4] = total

            @pl.when(owner % 4 != x_here)
            def _():
                wsend[owner] = total.astype(BF)
                x_copy(owner, x_here).start()

    def row_share(block):
        to_y = block // 2

        @pl.when(block % 2 == x_here // 2)
        def _():
            for j in range(1, 4):
                sender = (x_here + j) % 4
                x_copy(to_y * 4 + x_here, sender).wait_recv()
            total = wrow[to_y]
            for j in range(1, 4):
                total = total + wrecv[to_y, (x_here + j) % 4].astype(F32)

            @pl.when(to_y == y_here)
            def _():
                wmine[...] = total

            @pl.when(to_y != y_here)
            def _():
                ysend[to_y] = total.astype(BF)
                y_copy(to_y, y_here).start()

    def nth_block(n):
        return (z + NZ + (1 - 2 * (n % 2)) * ((n + 1) // 2)) % NZ

    def blocks(first, last):
        def one(n, carry):
            block_terms(nth_block(n), n % 2)
            block_share(nth_block(n - 1), (n - 1) % 2)
            return carry

        lax.fori_loop(first, last, one, 0)

    block_terms(z, 0, first=True)
    ag_forward(3)
    blocks(1, 3)
    ag_forward(4)

    def mixed_part(block, chunk):
        return dot(attn[rows_of(chunk * HALF, HALF), :], wb[block])

    def rs_copy(d, i):
        return pltpu.make_async_remote_copy(
            src_ref=rss.at[d, i], dst_ref=rsr.at[d, i],
            send_sem=rs_s.at[d, i], recv_sem=rs_r.at[d, i],
            device_id={"head": (z + 1) % NZ if d == 0 else (z + NZ - 1) % NZ},
            device_id_type=MESH,
        )

    def rs_part(d, i):
        distance = 4 - (i + 1) // 2
        block = (z + distance) % NZ if d == 0 else (z + NZ - distance) % NZ
        return mixed_part(block, ag_chunk(d, i))

    def rs_relay(i):
        for d in range(2):
            held[d] = rs_part(d, i + 2)
        for d in range(2):
            rs_copy(d, i).wait_recv()
            rss[d, i + 2] = (held[d] + rsr[d, i].astype(F32)).astype(BF)
            rs_copy(d, i + 2).start()

    for i in range(2):
        for d in range(2):
            rss[d, i] = rs_part(d, i).astype(BF)
            rs_copy(d, i).start()

    lmsib_copy.wait()
    lm2[0] = jnp.maximum(lmt[...], lmsib[...])

    def lm_copy(stage, to, slot):
        chip_to = y_here * 4 + to if stage == 0 else to * 4 + x_here
        return pltpu.make_async_remote_copy(
            src_ref=lm2.at[stage], dst_ref=lmr.at[stage, slot],
            send_sem=lm_s.at[stage, to], recv_sem=lm_r.at[stage, slot],
            device_id={"ctx": chip_to * 2 + core}, device_id_type=MESH,
        )

    places = (x_here, y_here)

    def lm_start(stage):
        for j in range(1, 4):
            lm_copy(stage, (places[stage] + j) % 4, places[stage]).start()

    def lm_gather(stage):
        total = lm2[stage]
        for j in range(1, 4):
            slot = (places[stage] + j) % 4
            lm_copy(stage, slot, slot).wait_recv()
            total = jnp.maximum(total, lmr[stage, slot])
        return total

    lm_start(0)

    blocks(3, 5)
    for d in range(2):
        ag_arrive(d, 5)
    blocks(5, 7)
    for d in range(2):
        ag_arrive(d, 6)
    blocks(7, 8)

    def permute_grad(b, carry):
        at = rows_of(b * BLK, BLK)
        gp[at, :] = dot(perm[...], gacc[at, :].astype(BF)).astype(BF)
        return carry

    lax.fori_loop(0, 4, permute_grad, 0)
    block_share(nth_block(7), 1)

    rsc, dq, rg = pk, tt, nm

    def score_grads(h, level, at, e, queries, keys, values):
        grad = rg[h, at, :].astype(BF)
        weights = dot_nt(grad, values)
        dz = (e * (weights - rsc[h, at, :][:, :1])).astype(BF)
        dq[h, at, :] = dot(dz, keys) * (SCALE * 0.5**level)
        return dot_tn(dz, queries) * SCALE, dot_tn(e.astype(BF), grad)

    def far_backward(h, carry):
        hs = lanes(h)

        def spread(b, inner):
            at = rows_of(b * BLK, BLK)
            g = gp[at, hs].astype(F32)
            delta = jnp.sum(g * af[h, at, :], axis=-1, keepdims=True)
            g = g.reshape(16, 8, DH)
            delta = jnp.broadcast_to(delta, (BLK, DH)).reshape(16, 8, DH)
            for level in range(LEVELS):
                share = wts5[h, level, at, :].reshape(16, 8, DH)
                grads, scalars = share * g, share * delta
                for _ in range(level):
                    grads, scalars = halve(grads), halve(scalars)
                n = BLK >> level
                put = rows_of(OFF[level] + b * n, n)
                rg[h, put, :] = grads.reshape(n, DH)
                rsc[h, put, :] = scalars.reshape(n, DH)
            return inner

        lax.fori_loop(0, 4, spread, 0)
        for level, queries, store in ((2, qc2, e2), (3, qc3, e3), (4, qc4, e4)):
            dk, dv = score_grads(
                h, level, pl.ds(OFF[level], TOK >> level), store[h],
                queries[:, hs], kvr[level - 2, 0, :, hs], kvr[level - 2, 1, :, hs],
            )
            gks[level - 2, 0, :, hs] = (dk * 0.5**level).astype(BF)
            gks[level - 2, 1, :, hs] = (dv * 0.5**level).astype(BF)
        return carry

    lax.fori_loop(0, 2, far_backward, 0)
    rs_relay(0)
    lax.fori_loop(2, HEADS, far_backward, 0)

    gk_sends = []
    for m in range(1, 8):
        if m == 1:
            src, dst, slot = gks.at[0], gkr2, 0
        elif m < 4:
            src = gks.at[1, :, rows_of(flipped(m) % 2 * 64, 64), :]
            dst, slot = gkr3.at[core], 1 + core
        else:
            src = gks.at[2, :, rows_of(flipped(m) % 4 * 32, 32), :]
            dst, slot = gkr4.at[c % 4], 3 + c % 4
        copy = pltpu.make_async_remote_copy(
            src_ref=src, dst_ref=dst, send_sem=gk_s.at[m], recv_sem=gk_r.at[slot],
            device_id={"ctx": flipped(m)}, device_id_type=MESH,
        )
        copy.start()
        gk_sends.append(copy)

    def near_backward(h, carry):
        hs = lanes(h)
        for p in range(2):
            at = pl.ds(p * 256, 256)
            dk, dv = score_grads(
                h, 0, at, e0[h, p], qkvp[0, at, hs], qkvp[1, at, hs], qkvp[2, at, hs]
            )
            gkp[at, hs] = dk
            gvp[at, hs] = dv
        for g in range(2):
            other = pl.ds((1 - g) * 128, 128)
            dk, dv = score_grads(
                h, 1, pl.ds(OFF[1] + g * 128, 128), e1[h, g],
                pool1[0, pl.ds(g * 128, 128), hs], pool1[1, other, hs], pool1[2, other, hs],
            )
            to = pl.ds((1 - g) * 256, 256)
            for ref, part in ((gkp, dk), (gvp, dv)):
                wide = expand((part * 0.5).reshape(16, 8, DH), 32).reshape(256, DH)
                ref[to, hs] = ref[to, hs] + wide

        def gather_q(b, inner):
            total = dq[h, rows_of(b * BLK, BLK), :].reshape(16, 8, DH)
            for level in range(1, LEVELS):
                n = BLK >> level
                part = dq[h, rows_of(OFF[level] + b * n, n), :].reshape(n // 8, 8, DH)
                total = total + expand(part, 16)
            gqp[rows_of(b * BLK, BLK), hs] = total.reshape(BLK, DH)
            return inner

        lax.fori_loop(0, 4, gather_q, 0)
        return carry

    def row_shares(first, last):
        def one(n, carry):
            row_share(nth_block(n))
            return carry

        lax.fori_loop(first, last, one, 0)

    lax.fori_loop(0, 2, near_backward, 0)
    rs_relay(1)
    row_shares(0, 3)
    lm2[1] = lm_gather(0)
    lm_start(1)
    lax.fori_loop(2, HEADS, near_backward, 0)
    rs_relay(2)
    row_shares(3, 7)

    def token_order(ref, b):
        at = rows_of(b * BLK, BLK)
        x = ref[at, :]
        high = x.astype(BF)
        low = (x - high.astype(F32)).astype(BF)
        ref[at, :] = dot(unperm[...], high) + dot(unperm[...], low)

    def finish_q(b, carry):
        token_order(gqp, b)
        return carry

    lax.fori_loop(0, 4, finish_q, 0)
    mix[pl.ds(0, HALF), :] = mixed_part(z, 0)
    mix[pl.ds(HALF, HALF), :] = mixed_part(z, 1)
    rs_relay(3)
    row_shares(7, 8)

    for slot in range(7):
        if slot == 0:
            src, dst = gks.at[0], gkr2
        elif slot < 3:
            src, dst = gks.at[1, :, pl.ds(0, 64), :], gkr3.at[slot - 1]
        else:
            src, dst = gks.at[2, :, pl.ds(0, 32), :], gkr4.at[slot - 3]
        pltpu.make_async_remote_copy(
            src_ref=src, dst_ref=dst, send_sem=gk_s.at[1], recv_sem=gk_r.at[slot],
            device_id={"ctx": flipped(1)}, device_id_type=MESH,
        ).wait_recv()

    for t, own in enumerate((gkp, gvp)):
        p4[t] = sum(gkr4[s, t].astype(F32) for s in range(4))

        def finish_kv(b, carry, t=t, own=own):
            at = rows_of(b * BLK, BLK)
            two = gkr2[t, rows_of(b * 32, 32), :].astype(F32)
            three = gkr3[0, t, rows_of(b * 16, 16), :].astype(F32)
            three = three + gkr3[1, t, rows_of(b * 16, 16), :].astype(F32)
            four = p4[t, rows_of(b * 8, 8), :]
            low = expand(three.reshape(2, 8, WID), 4) + expand(four.reshape(1, 8, WID), 4)
            low = low + two.reshape(4, 8, WID)
            own[at, :] = own[at, :] + expand(low, 16).reshape(BLK, WID)
            token_order(own, b)
            return carry

        lax.fori_loop(0, 4, finish_kv, 0)

    rs_relay(4)

    for j in range(1, 4):
        y_copy(y_here, (y_here + j) % 4).wait_recv()
    total = wmine[...]
    for j in range(1, 4):
        total = total + yrecv[(y_here + j) % 4].astype(F32)
    wmine[...] = total

    lm_out[...] = lm_gather(1)[:HEADS, :LEVELS]

    for copy in kv_sends + gk_sends:
        copy.wait_send()

    def drain(i, carry):
        for d in range(2):
            ag_send(d, i).wait_send()
            rs_copy(d, i).wait_send()
        return carry

    lax.fori_loop(0, 7, drain, 0)

    def drain_sib(i, carry):
        sib_copy(i).wait_send()
        return carry

    lax.fori_loop(0, NZ, drain_sib, 0)

    def drain_chips(j, carry):
        to = (chip + j) % CHIPS

        @pl.when(to % 4 != x_here)
        def _():
            x_copy(to, x_here).wait_send()

        return carry

    lax.fori_loop(1, CHIPS, drain_chips, 0)
    for j in range(1, 4):
        y_copy((y_here + j) % 4, y_here).wait_send()
        for stage in range(2):
            lm_copy(stage, (places[stage] + j) % 4, places[stage]).wait_send()

    for i, chunks in ((5, (1, 0)), (6, (0, 1))):
        for d in range(2):
            rs_copy(d, i).wait_recv()
            at = pl.ds(chunks[d] * HALF, HALF)
            mix[at, :] = mix[at, :] + rsr[d, i].astype(F32)


def finish(*refs):
    sems = refs[-1]
    copies = []
    for t in range(6):
        pieces = 2 if t == 0 else 1
        size = refs[t].shape[0] // pieces
        for piece in range(pieces):
            at = pl.ds(piece * size, size)
            copies.append(
                pltpu.make_async_copy(
                    refs[t].at[at, :], refs[6 + t].at[at, :], sems.at[len(copies)]
                )
            )
    for copy in copies:
        copy.start()
    for copy in copies:
        copy.wait()


def vmem(shape, kind):
    return pltpu.VMEM(shape, kind)


def per_device(query_input, key_input, value_input, out_weight, out_cotangent):
    dma = pltpu.SemaphoreType.DMA
    scratch = [
        vmem((3, TOK, WID), BF),
        vmem((BLK, BLK), BF),
        vmem((BLK, BLK), BF),
        vmem((3, TOK, WID), BF),
        vmem((3, 256, WID), BF),
        vmem((128, WID), BF),
        vmem((64, WID), BF),
        vmem((3, 32, WID), F32),
        vmem((32, WID), BF),
        vmem((2, 128, WID), BF),
        vmem((2, 64, WID), BF),
        vmem((2, 32, WID), BF),
        vmem((3, 2, 128, WID), BF),
        vmem((HEADS, 2, 256, 256), F32),
        vmem((HEADS, 2, 128, 128), F32),
        vmem((HEADS, 128, 128), F32),
        vmem((HEADS, 64, 128), F32),
        vmem((HEADS, 32, 128), F32),
        vmem((HEADS, ROWS, DH), F32),
        vmem((HEADS, ROWS, DH), F32),
        vmem((HEADS, ROWS, DH), F32),
        vmem((HEADS, LEVELS, TOK, DH), F32),
        vmem((HEADS, TOK, DH), F32),
        vmem((TOK, WID), BF),
        vmem((TOK, WID), BF),
        vmem((WID, TOK), BF),
        vmem((NZ, TOK, WID), BF),
        vmem((NZ, WID, WID), BF),
        vmem((TOK, WID), F32),
        vmem((TOK, WID), BF),
        vmem((4, HALF, DH), F32),
        vmem((2, 2, WID, DH), F32),
        vmem((NZ, 2, WID, DH), BF),
        vmem((NZ, 2, WID, DH), BF),
        vmem((CHIPS, WID, DH), BF),
        vmem((4, 4, WID, DH), BF),
        vmem((4, WID, DH), F32),
        vmem((4, WID, DH), BF),
        vmem((4, WID, DH), BF),
        vmem((2, 7, HALF, WID), BF),
        vmem((2, 7, HALF, WID), BF),
        vmem((2, HALF, WID), F32),
        vmem((3, 2, 128, WID), BF),
        vmem((2, 128, WID), BF),
        vmem((2, 2, 64, WID), BF),
        vmem((4, 2, 32, WID), BF),
        vmem((8, DH), F32),
        vmem((8, DH), F32),
        vmem((2, 8, DH), F32),
        vmem((2, 4, 8, DH), F32),
        dma((3,)), dma((NZ,)), dma,
        dma((2, 7)), dma((2, 7)),
        dma((8,)), dma((7,)), dma((8,)), dma((7,)),
        dma((NZ,)), dma((NZ,)), dma((CHIPS,)), dma((4, 4)), dma((4,)), dma((4,)),
        dma((2, 7)), dma((2, 7)),
        dma, dma, dma((2, 4)), dma((2, 4)),
    ]
    outs = pl.pallas_call(
        kernel,
        out_shape=tuple(vmem((TOK, WID), F32) for _ in range(4))
        + (vmem((WID, DH), F32), vmem((HEADS, LEVELS), F32)),
        in_specs=[pl.BlockSpec(memory_space=pl.ANY)] * 5,
        out_specs=[pl.BlockSpec(memory_space=pltpu.VMEM)] * 6,
        scratch_shapes=scratch,
        compiler_params=pltpu.CompilerParams(
            collective_id=0, has_side_effects=True, vmem_limit_bytes=56000000
        ),
        name="layer",
    )(query_input, key_input, value_input, out_weight, out_cotangent)
    held = [pltpu.with_memory_space_constraint(x, pltpu.VMEM) for x in outs]
    anywhere = pl.BlockSpec(memory_space=pl.ANY)
    local = pl.BlockSpec(memory_space=pltpu.VMEM)
    wide = jax.ShapeDtypeStruct((TOK, WID), F32)
    outs = pl.pallas_call(
        finish,
        out_shape=(
            wide, wide, wide, wide,
            jax.ShapeDtypeStruct((WID, DH), F32),
            jax.ShapeDtypeStruct((HEADS, LEVELS), F32),
        ),
        in_specs=[local] * 6,
        out_specs=[anywhere] * 6,
        scratch_shapes=[dma((18,))],
        compiler_params=pltpu.CompilerParams(vmem_limit_bytes=1000000),
        name="finish",
    )(*held)
    return outs[:5] + (outs[5].T,)


def solution(mesh):
    in_specs = (
        P("ctx", "head"),
        P("ctx", "head"),
        P("ctx", "head"),
        P("head", None),
        P("ctx", "head"),
    )
    out_specs = (
        P("ctx", "head"),
        P("ctx", "head"),
        P("ctx", "head"),
        P("ctx", "head"),
        P("head", "ctx"),
        P(None, "head"),
    )
    return jax.shard_map(
        per_device, mesh=mesh, in_specs=in_specs, out_specs=out_specs, check_vma=False
    )
```

```python
import functools
import math

import jax
import jax.numpy as jnp
from jax import lax
from jax.experimental import pallas as pl
from jax.experimental.pallas import tpu as pltpu
from jax.sharding import PartitionSpec as P

DH = 128
BLK = 128
LEVELS = 5
NZ = 8
NCTX = 32
CHIPS = 16
HEADS = 4
TOK = 512
WID = HEADS * DH
HALF = TOK // 2
LOG_TWO = math.log(2.0)
SCALE = DH ** (-0.5)
MESH = pl.DeviceIdType.MESH
BF = jnp.bfloat16
F32 = jnp.float32
OFF = (0, 512, 768, 896, 960)
ROWS = 992


def dot(a, b):
    return lax.dot_general(a, b, (((1,), (0,)), ((), ())), preferred_element_type=F32)


def dot_nt(a, b):
    return lax.dot_general(a, b, (((1,), (1,)), ((), ())), preferred_element_type=F32)


def dot_tn(a, b):
    return lax.dot_general(a, b, (((0,), (0,)), ((), ())), preferred_element_type=F32)


def rows_of(start, size):
    return pl.ds(pl.multiple_of(start, size), size)


def expand(x, slabs):
    n = x.shape[0]
    if n == slabs:
        return x
    return jnp.broadcast_to(x[:, None], (n, slabs // n, 8, x.shape[2])).reshape(
        slabs, 8, x.shape[2]
    )


def halve(x):
    y = x.reshape(x.shape[0] // 2, 2, 8, x.shape[2])
    return y[:, 0] + y[:, 1]


def kernel(
    q_in, k_in, v_in, w_in, c_in,
    mix, gqp, gkp, gvp, wmine, lm_out,
    qkv, perm, unperm, qkvp, pool1, qc2, qc3, p4, qc4, kvs2, kvs3, kvs4, kvr,
    e0, e1, e2, e3, e4, pk, tt, nm, wts5, af, ap, attn, attnt,
    cotg, wb, gacc, gp, wtile, wown, sibs, sibr, wsend, wrecv, wrow, ysend, yrecv,
    rss, rsr, held, gks, gkr2, gkr3, gkr4, lmt, lmsib, lm2, lmr,
    in_sem, w_sem, c_sem, ag_s, ag_r, kv_s, kv_r, gk_s, gk_r,
    sib_s, sib_r, w_s, w_r, y_s, y_r, rs_s, rs_r, lmsib_s, lmsib_r, lm_s, lm_r,
):
    c = lax.axis_index("ctx")
    z = lax.axis_index("head")
    core = c % 2
    chip = c // 2
    x_here, y_here = chip % 4, chip // 4

    def flipped(m):
        out = c
        for bit in range(3):
            if m >> bit & 1:
                out = out + (1 - 2 * (c // 2**bit % 2)) * 2**bit
        return out

    barrier = pltpu.get_barrier_semaphore()
    for step in (1, NZ - 1):
        pl.semaphore_signal(
            barrier, inc=1, device_id={"head": (z + step) % NZ}, device_id_type=MESH
        )
    for m in range(1, 8):
        pl.semaphore_signal(barrier, inc=1, device_id={"ctx": flipped(m)}, device_id_type=MESH)

    for j in range(1, 4):
        pl.semaphore_signal(
            barrier,
            inc=1,
            device_id={"ctx": ((y_here + j) % 4 * 4 + x_here) * 2 + core},
            device_id_type=MESH,
        )
    c_copy = pltpu.make_async_copy(c_in, cotg.at[z], c_sem)
    c_copy.start()
    in_copies = [
        pltpu.make_async_copy(src, qkv.at[t], in_sem.at[t])
        for t, src in enumerate((q_in, k_in, v_in))
    ]
    for copy in in_copies:
        copy.start()
    w_copies = [
        pltpu.make_async_copy(w_in.at[:, pl.ds(j * WID, WID)], wb.at[j], w_sem.at[j])
        for j in range(NZ)
    ]

    pl.semaphore_wait(barrier, 2 + 7 + 3)

    def ag_region(d, block, chunk):
        return cotg.at[block, rows_of(chunk * HALF, HALF), :]

    def ag_chunk(d, i):
        return i % 2 if d == 0 else 1 - i % 2

    def ag_send(d, i):
        if d == 0:
            block, to = (z + NZ - i // 2) % NZ, (z + 1) % NZ
        else:
            block, to = (z + i // 2) % NZ, (z + NZ - 1) % NZ
        region = ag_region(d, block, ag_chunk(d, i))
        return pltpu.make_async_remote_copy(
            src_ref=region, dst_ref=region, send_sem=ag_s.at[d, i], recv_sem=ag_r.at[d, i],
            device_id={"head": to}, device_id_type=MESH,
        )

    def own_send(d, i):
        chunk = i if d == 0 else 1 - i
        return pltpu.make_async_remote_copy(
            src_ref=c_in.at[pl.ds(chunk * HALF, HALF), :], dst_ref=ag_region(d, z, chunk),
            send_sem=ag_s.at[d, i], recv_sem=ag_r.at[d, i],
            device_id={"head": (z + 1) % NZ if d == 0 else (z + NZ - 1) % NZ},
            device_id_type=MESH,
        )

    def ag_arrive(d, i):
        if d == 0:
            block = (z + 2 * NZ - 1 - i // 2) % NZ
        else:
            block = (z + 1 + i // 2) % NZ
        region = ag_region(d, block, ag_chunk(d, i))
        pltpu.make_async_remote_copy(
            src_ref=region, dst_ref=region, send_sem=ag_s.at[d, i], recv_sem=ag_r.at[d, i],
            device_id={"head": (z + 1) % NZ}, device_id_type=MESH,
        ).wait_recv()

    def ag_forward(i):
        for d in range(2):
            ag_arrive(d, i)
            ag_send(d, i + 2).start()

    for i in range(2):
        for d in range(2):
            own_send(d, i).start()
    for copy in w_copies:
        copy.start()
    c_copy.wait()

    row_id = lax.broadcasted_iota(jnp.int32, (BLK, BLK), 0)
    col_id = lax.broadcasted_iota(jnp.int32, (BLK, BLK), 1)
    perm[...] = jnp.where(col_id == row_id % 8 * 16 + row_id // 8, 1.0, 0.0).astype(BF)
    unperm[...] = jnp.where(row_id == col_id % 8 * 16 + col_id // 8, 1.0, 0.0).astype(BF)
    lmt[...] = jnp.full((8, DH), -3.0e38, F32)

    for t in (1, 2, 0):
        in_copies[t].wait()

        def pool(b, carry, t=t):
            x = dot(perm[...], qkv[t, rows_of(b * BLK, BLK), :])
            qkvp[t, rows_of(b * BLK, BLK), :] = x.astype(BF)
            one = halve(x.reshape(16, 8, WID))
            pool1[t, rows_of(b * 64, 64), :] = (one * 0.5).reshape(64, WID).astype(BF)
            two = halve(one)
            two_rows = (two * 0.25).reshape(32, WID).astype(BF)
            three = halve(two)
            three_rows = (three * 0.125).reshape(16, WID).astype(BF)
            if t == 0:
                qc2[rows_of(b * 32, 32), :] = two_rows
                qc3[rows_of(b * 16, 16), :] = three_rows
            else:
                kvs2[t - 1, rows_of(b * 32, 32), :] = two_rows
                kvs3[t - 1, rows_of(b * 16, 16), :] = three_rows
            p4[t, rows_of(b * 8, 8), :] = (halve(three) * 0.0625).reshape(8, WID)
            return carry

        lax.fori_loop(0, 4, pool, 0)
        if t == 0:
            qc4[...] = p4[0].astype(BF)
        else:
            kvs4[t - 1] = p4[t].astype(BF)

        if t == 2:
            kv_sends = []
            for m in range(1, 8):
                if m == 1:
                    src, dst, slot = kvs2, kvr.at[0], 0
                elif m < 4:
                    src, slot = kvs3, 1 + core
                    dst = kvr.at[1, :, rows_of(core * 64, 64), :]
                else:
                    src, slot = kvs4, 3 + c % 4
                    dst = kvr.at[2, :, rows_of(c % 4 * 32, 32), :]
                copy = pltpu.make_async_remote_copy(
                    src_ref=src, dst_ref=dst, send_sem=kv_s.at[m], recv_sem=kv_r.at[slot],
                    device_id={"ctx": flipped(m)}, device_id_type=MESH,
                )
                copy.start()
                kv_sends.append(copy)

    def kv_arrive():
        for slot in range(7):
            if slot == 0:
                src, dst = kvs2, kvr.at[0]
            elif slot < 3:
                src, dst = kvs3, kvr.at[1, :, pl.ds((slot - 1) * 64, 64), :]
            else:
                src, dst = kvs4, kvr.at[2, :, pl.ds((slot - 3) * 32, 32), :]
            pltpu.make_async_remote_copy(
                src_ref=src, dst_ref=dst, send_sem=kv_s.at[1], recv_sem=kv_r.at[slot],
                device_id={"ctx": flipped(1)}, device_id_type=MESH,
            ).wait_recv()

    tile_row = lax.broadcasted_iota(jnp.int32, (8, DH), 0)
    tile_col = lax.broadcasted_iota(jnp.int32, (8, DH), 1)

    def attend(h, level, start, count, queries, keys, values):
        scores = dot_nt(queries, keys) * SCALE
        peak = jnp.max(scores, axis=-1, keepdims=True)
        e = jnp.exp(scores - peak)
        total = jnp.sum(e, axis=-1, keepdims=True)
        wide = jnp.broadcast_to(peak, (count, DH))
        at = pl.ds(start, count) if isinstance(start, int) else start
        pk[h, at, :] = wide + level * LOG_TWO
        tt[h, at, :] = jnp.broadcast_to(total, (count, DH))
        nm[h, at, :] = dot(e.astype(BF), values)
        top = jnp.max(wide.reshape(count // 8, 8, DH), axis=0)
        top = jnp.broadcast_to(jnp.max(top, axis=0, keepdims=True), (8, DH))
        here = jnp.logical_and(tile_row == h, tile_col == level)
        lmt[...] = jnp.where(here, jnp.maximum(lmt[...], top), lmt[...])
        return e

    def lanes(h):
        return rows_of(h * DH, DH)

    def near_forward(h, carry):
        hs = lanes(h)
        for p in range(2):
            at = pl.ds(p * 256, 256)
            e0[h, p] = attend(h, 0, p * 256, 256, qkvp[0, at, hs], qkvp[1, at, hs], qkvp[2, at, hs])
        for g in range(2):
            other = pl.ds((1 - g) * 128, 128)
            e1[h, g] = attend(
                h, 1, OFF[1] + g * 128, 128,
                pool1[0, pl.ds(g * 128, 128), hs], pool1[1, other, hs], pool1[2, other, hs],
            )
        return carry

    lax.fori_loop(0, 2, near_forward, 0)
    ag_forward(0)
    lax.fori_loop(2, HEADS, near_forward, 0)
    ag_forward(1)
    kv_arrive()

    def far_forward(h, carry):
        hs = lanes(h)
        for level, queries, store in ((2, qc2, e2), (3, qc3, e3), (4, qc4, e4)):
            count = TOK >> level
            store[h] = attend(
                h, level, OFF[level], count,
                queries[:, hs], kvr[level - 2, 0, :, hs], kvr[level - 2, 1, :, hs],
            )

        def merge(b, inner):
            def level_rows(ref, level):
                n = BLK >> level
                return expand(ref[h, rows_of(OFF[level] + b * n, n), :].reshape(n // 8, 8, DH), 16)

            peaks = [level_rows(pk, level) for level in range(LEVELS)]
            highest = peaks[0]
            for other in peaks[1:]:
                highest = jnp.maximum(highest, other)
            scales = [jnp.exp(peak - highest) for peak in peaks]
            den = scales[0] * level_rows(tt, 0)
            num = scales[0] * level_rows(nm, 0)
            for level in range(1, LEVELS):
                den = den + scales[level] * level_rows(tt, level)
                num = num + scales[level] * level_rows(nm, level)
            inv = 1.0 / den
            at = rows_of(b * BLK, BLK)
            for level in range(LEVELS):
                wts5[h, level, at, :] = (scales[level] * inv).reshape(BLK, DH)
            out = (num * inv).reshape(BLK, DH)
            af[h, at, :] = out
            ap[at, hs] = out.astype(BF)
            return inner

        lax.fori_loop(0, 4, merge, 0)
        return carry

    lax.fori_loop(0, HEADS, far_forward, 0)
    ag_forward(2)

    lmsib_copy = pltpu.make_async_remote_copy(
        src_ref=lmt, dst_ref=lmsib, send_sem=lmsib_s, recv_sem=lmsib_r,
        device_id={"ctx": flipped(1)}, device_id_type=MESH,
    )
    lmsib_copy.start()

    def restore(b, carry):
        at = rows_of(b * BLK, BLK)
        attn[at, :] = dot(unperm[...], ap[at, :]).astype(BF)
        return carry

    lax.fori_loop(0, 4, restore, 0)

    def turn(f, carry):
        attnt[rows_of(f * DH, DH), :] = attn[:, rows_of(f * DH, DH)].astype(F32).T.astype(BF)
        return carry

    lax.fori_loop(0, HEADS, turn, 0)
    for copy in w_copies:
        copy.wait()

    def sib_copy(block):
        return pltpu.make_async_remote_copy(
            src_ref=sibs.at[block], dst_ref=sibr.at[block],
            send_sem=sib_s.at[block], recv_sem=sib_r.at[block],
            device_id={"ctx": flipped(1)}, device_id_type=MESH,
        )

    def x_copy(owner, sender):
        return pltpu.make_async_remote_copy(
            src_ref=wsend.at[owner], dst_ref=wrecv.at[owner // 4, sender],
            send_sem=w_s.at[owner], recv_sem=w_r.at[owner // 4, sender],
            device_id={"ctx": (y_here * 4 + owner % 4) * 2 + core}, device_id_type=MESH,
        )

    def y_copy(to_y, sender):
        return pltpu.make_async_remote_copy(
            src_ref=ysend.at[to_y], dst_ref=yrecv.at[sender],
            send_sem=y_s.at[to_y], recv_sem=y_r.at[sender],
            device_id={"ctx": (to_y * 4 + x_here) * 2 + core}, device_id_type=MESH,
        )

    def block_terms(block, slot, first=False):
        def part(r, carry):
            at = rows_of(r * HALF, HALF)
            term = dot_nt(cotg[block, at, :], wb[block])
            gacc[at, :] = term if first else gacc[at, :] + term
            weight = dot(attnt[at, :], cotg[block])
            for m in range(4):
                wtile[m] = weight[:, m * DH : (m + 1) * DH]
            for i in range(2):
                wown[slot, i, at, :] = wtile[2 * i + core]
                sibs[block, i, at, :] = wtile[2 * i + 1 - core].astype(BF)
            return carry

        lax.fori_loop(0, 2, part, 0)
        sib_copy(block).start()

    def block_share(block, slot):
        sib_copy(block).wait_recv()
        for i in range(2):
            owner = 2 * block + i
            total = wown[slot, i] + sibr[block, i].astype(F32)

            @pl.when(owner % 4 == x_here)
            def _():
                wrow[owner // 4] = total

            @pl.when(owner % 4 != x_here)
            def _():
                wsend[owner] = total.astype(BF)
                x_copy(owner, x_here).start()

    def row_share(block):
        to_y = block // 2

        @pl.when(block % 2 == x_here // 2)
        def _():
            for j in range(1, 4):
                sender = (x_here + j) % 4
                x_copy(to_y * 4 + x_here, sender).wait_recv()
            total = wrow[to_y]
            for j in range(1, 4):
                total = total + wrecv[to_y, (x_here + j) % 4].astype(F32)

            @pl.when(to_y == y_here)
            def _():
                wmine[...] = total

            @pl.when(to_y != y_here)
            def _():
                ysend[to_y] = total.astype(BF)
                y_copy(to_y, y_here).start()

    def nth_block(n):
        return (z + NZ + (1 - 2 * (n % 2)) * ((n + 1) // 2)) % NZ

    def blocks(first, last):
        def one(n, carry):
            block_terms(nth_block(n), n % 2)
            block_share(nth_block(n - 1), (n - 1) % 2)
            return carry

        lax.fori_loop(first, last, one, 0)

    block_terms(z, 0, first=True)
    ag_forward(3)
    blocks(1, 3)
    ag_forward(4)

    def mixed_part(block, chunk):
        return dot(attn[rows_of(chunk * HALF, HALF), :], wb[block])

    def rs_copy(d, i):
        return pltpu.make_async_remote_copy(
            src_ref=rss.at[d, i], dst_ref=rsr.at[d, i],
            send_sem=rs_s.at[d, i], recv_sem=rs_r.at[d, i],
            device_id={"head": (z + 1) % NZ if d == 0 else (z + NZ - 1) % NZ},
            device_id_type=MESH,
        )

    def rs_part(d, i):
        distance = 4 - (i + 1) // 2
        block = (z + distance) % NZ if d == 0 else (z + NZ - distance) % NZ
        return mixed_part(block, ag_chunk(d, i))

    def rs_relay(i):
        for d in range(2):
            held[d] = rs_part(d, i + 2)
        for d in range(2):
            rs_copy(d, i).wait_recv()
            rss[d, i + 2] = (held[d] + rsr[d, i].astype(F32)).astype(BF)
            rs_copy(d, i + 2).start()

    for i in range(2):
        for d in range(2):
            rss[d, i] = rs_part(d, i).astype(BF)
            rs_copy(d, i).start()

    lmsib_copy.wait()
    lm2[0] = jnp.maximum(lmt[...], lmsib[...])

    def lm_copy(stage, to, slot):
        chip_to = y_here * 4 + to if stage == 0 else to * 4 + x_here
        return pltpu.make_async_remote_copy(
            src_ref=lm2.at[stage], dst_ref=lmr.at[stage, slot],
            send_sem=lm_s.at[stage, to], recv_sem=lm_r.at[stage, slot],
            device_id={"ctx": chip_to * 2 + core}, device_id_type=MESH,
        )

    places = (x_here, y_here)

    def lm_start(stage):
        for j in range(1, 4):
            lm_copy(stage, (places[stage] + j) % 4, places[stage]).start()

    def lm_gather(stage):
        total = lm2[stage]
        for j in range(1, 4):
            slot = (places[stage] + j) % 4
            lm_copy(stage, slot, slot).wait_recv()
            total = jnp.maximum(total, lmr[stage, slot])
        return total

    lm_start(0)

    blocks(3, 5)
    for d in range(2):
        ag_arrive(d, 5)
    blocks(5, 7)
    for d in range(2):
        ag_arrive(d, 6)
    blocks(7, 8)

    def permute_grad(b, carry):
        at = rows_of(b * BLK, BLK)
        gp[at, :] = dot(perm[...], gacc[at, :].astype(BF)).astype(BF)
        return carry

    lax.fori_loop(0, 4, permute_grad, 0)
    block_share(nth_block(7), 1)

    rsc, dq, rg = pk, tt, nm

    def score_grads(h, level, at, e, queries, keys, values):
        grad = rg[h, at, :].astype(BF)
        weights = dot_nt(grad, values)
        dz = (e * (weights - rsc[h, at, :][:, :1])).astype(BF)
        dq[h, at, :] = dot(dz, keys) * (SCALE * 0.5**level)
        return dot_tn(dz, queries) * SCALE, dot_tn(e.astype(BF), grad)

    def far_backward(h, carry):
        hs = lanes(h)

        def spread(b, inner):
            at = rows_of(b * BLK, BLK)
            g = gp[at, hs].astype(F32)
            delta = jnp.sum(g * af[h, at, :], axis=-1, keepdims=True)
            g = g.reshape(16, 8, DH)
            delta = jnp.broadcast_to(delta, (BLK, DH)).reshape(16, 8, DH)
            for level in range(LEVELS):
                share = wts5[h, level, at, :].reshape(16, 8, DH)
                grads, scalars = share * g, share * delta
                for _ in range(level):
                    grads, scalars = halve(grads), halve(scalars)
                n = BLK >> level
                put = rows_of(OFF[level] + b * n, n)
                rg[h, put, :] = grads.reshape(n, DH)
                rsc[h, put, :] = scalars.reshape(n, DH)
            return inner

        lax.fori_loop(0, 4, spread, 0)
        for level, queries, store in ((2, qc2, e2), (3, qc3, e3), (4, qc4, e4)):
            dk, dv = score_grads(
                h, level, pl.ds(OFF[level], TOK >> level), store[h],
                queries[:, hs], kvr[level - 2, 0, :, hs], kvr[level - 2, 1, :, hs],
            )
            gks[level - 2, 0, :, hs] = (dk * 0.5**level).astype(BF)
            gks[level - 2, 1, :, hs] = (dv * 0.5**level).astype(BF)
        return carry

    lax.fori_loop(0, 2, far_backward, 0)
    rs_relay(0)
    lax.fori_loop(2, HEADS, far_backward, 0)

    gk_sends = []
    for m in range(1, 8):
        if m == 1:
            src, dst, slot = gks.at[0], gkr2, 0
        elif m < 4:
            src = gks.at[1, :, rows_of(flipped(m) % 2 * 64, 64), :]
            dst, slot = gkr3.at[core], 1 + core
        else:
            src = gks.at[2, :, rows_of(flipped(m) % 4 * 32, 32), :]
            dst, slot = gkr4.at[c % 4], 3 + c % 4
        copy = pltpu.make_async_remote_copy(
            src_ref=src, dst_ref=dst, send_sem=gk_s.at[m], recv_sem=gk_r.at[slot],
            device_id={"ctx": flipped(m)}, device_id_type=MESH,
        )
        copy.start()
        gk_sends.append(copy)

    def near_backward(h, carry):
        hs = lanes(h)
        for p in range(2):
            at = pl.ds(p * 256, 256)
            dk, dv = score_grads(
                h, 0, at, e0[h, p], qkvp[0, at, hs], qkvp[1, at, hs], qkvp[2, at, hs]
            )
            gkp[at, hs] = dk
            gvp[at, hs] = dv
        for g in range(2):
            other = pl.ds((1 - g) * 128, 128)
            dk, dv = score_grads(
                h, 1, pl.ds(OFF[1] + g * 128, 128), e1[h, g],
                pool1[0, pl.ds(g * 128, 128), hs], pool1[1, other, hs], pool1[2, other, hs],
            )
            to = pl.ds((1 - g) * 256, 256)
            for ref, part in ((gkp, dk), (gvp, dv)):
                wide = expand((part * 0.5).reshape(16, 8, DH), 32).reshape(256, DH)
                ref[to, hs] = ref[to, hs] + wide

        def gather_q(b, inner):
            total = dq[h, rows_of(b * BLK, BLK), :].reshape(16, 8, DH)
            for level in range(1, LEVELS):
                n = BLK >> level
                part = dq[h, rows_of(OFF[level] + b * n, n), :].reshape(n // 8, 8, DH)
                total = total + expand(part, 16)
            gqp[rows_of(b * BLK, BLK), hs] = total.reshape(BLK, DH)
            return inner

        lax.fori_loop(0, 4, gather_q, 0)
        return carry

    def row_shares(first, last):
        def one(n, carry):
            row_share(nth_block(n))
            return carry

        lax.fori_loop(first, last, one, 0)

    lax.fori_loop(0, 2, near_backward, 0)
    rs_relay(1)
    row_shares(0, 3)
    lm2[1] = lm_gather(0)
    lm_start(1)
    lax.fori_loop(2, HEADS, near_backward, 0)
    rs_relay(2)
    row_shares(3, 7)

    def token_order(ref, b):
        at = rows_of(b * BLK, BLK)
        x = ref[at, :]
        high = x.astype(BF)
        low = (x - high.astype(F32)).astype(BF)
        ref[at, :] = dot(unperm[...], high) + dot(unperm[...], low)

    def finish_q(b, carry):
        token_order(gqp, b)
        return carry

    lax.fori_loop(0, 4, finish_q, 0)
    mix[pl.ds(0, HALF), :] = mixed_part(z, 0)
    mix[pl.ds(HALF, HALF), :] = mixed_part(z, 1)
    rs_relay(3)
    row_shares(7, 8)

    for slot in range(7):
        if slot == 0:
            src, dst = gks.at[0], gkr2
        elif slot < 3:
            src, dst = gks.at[1, :, pl.ds(0, 64), :], gkr3.at[slot - 1]
        else:
            src, dst = gks.at[2, :, pl.ds(0, 32), :], gkr4.at[slot - 3]
        pltpu.make_async_remote_copy(
            src_ref=src, dst_ref=dst, send_sem=gk_s.at[1], recv_sem=gk_r.at[slot],
            device_id={"ctx": flipped(1)}, device_id_type=MESH,
        ).wait_recv()

    for t, own in enumerate((gkp, gvp)):
        p4[t] = sum(gkr4[s, t].astype(F32) for s in range(4))

        def finish_kv(b, carry, t=t, own=own):
            at = rows_of(b * BLK, BLK)
            two = gkr2[t, rows_of(b * 32, 32), :].astype(F32)
            three = gkr3[0, t, rows_of(b * 16, 16), :].astype(F32)
            three = three + gkr3[1, t, rows_of(b * 16, 16), :].astype(F32)
            four = p4[t, rows_of(b * 8, 8), :]
            low = expand(three.reshape(2, 8, WID), 4) + expand(four.reshape(1, 8, WID), 4)
            low = low + two.reshape(4, 8, WID)
            own[at, :] = own[at, :] + expand(low, 16).reshape(BLK, WID)
            token_order(own, b)
            return carry

        lax.fori_loop(0, 4, finish_kv, 0)

    rs_relay(4)

    for j in range(1, 4):
        y_copy(y_here, (y_here + j) % 4).wait_recv()
    total = wmine[...]
    for j in range(1, 4):
        total = total + yrecv[(y_here + j) % 4].astype(F32)
    wmine[...] = total

    lm_out[...] = lm_gather(1)[:HEADS, :LEVELS]

    for copy in kv_sends + gk_sends:
        copy.wait_send()

    def drain(i, carry):
        for d in range(2):
            ag_send(d, i).wait_send()
            rs_copy(d, i).wait_send()
        return carry

    lax.fori_loop(0, 7, drain, 0)

    def drain_sib(i, carry):
        sib_copy(i).wait_send()
        return carry

    lax.fori_loop(0, NZ, drain_sib, 0)

    def drain_chips(j, carry):
        to = (chip + j) % CHIPS

        @pl.when(to % 4 != x_here)
        def _():
            x_copy(to, x_here).wait_send()

        return carry

    lax.fori_loop(1, CHIPS, drain_chips, 0)
    for j in range(1, 4):
        y_copy((y_here + j) % 4, y_here).wait_send()
        for stage in range(2):
            lm_copy(stage, (places[stage] + j) % 4, places[stage]).wait_send()

    for i, chunks in ((5, (1, 0)), (6, (0, 1))):
        for d in range(2):
            rs_copy(d, i).wait_recv()
            at = pl.ds(chunks[d] * HALF, HALF)
            mix[at, :] = mix[at, :] + rsr[d, i].astype(F32)


def finish(*refs):
    sems = refs[-1]
    copies = []
    for t in range(6):
        pieces = 2 if t == 0 else 1
        size = refs[t].shape[0] // pieces
        for piece in range(pieces):
            at = pl.ds(piece * size, size)
            copies.append(
                pltpu.make_async_copy(
                    refs[t].at[at, :], refs[6 + t].at[at, :], sems.at[len(copies)]
                )
            )
    for copy in copies:
        copy.start()
    for copy in copies:
        copy.wait()


def vmem(shape, kind):
    return pltpu.VMEM(shape, kind)


def per_device(query_input, key_input, value_input, out_weight, out_cotangent):
    dma = pltpu.SemaphoreType.DMA
    scratch = [
        vmem((3, TOK, WID), BF),
        vmem((BLK, BLK), BF),
        vmem((BLK, BLK), BF),
        vmem((3, TOK, WID), BF),
        vmem((3, 256, WID), BF),
        vmem((128, WID), BF),
        vmem((64, WID), BF),
        vmem((3, 32, WID), F32),
        vmem((32, WID), BF),
        vmem((2, 128, WID), BF),
        vmem((2, 64, WID), BF),
        vmem((2, 32, WID), BF),
        vmem((3, 2, 128, WID), BF),
        vmem((HEADS, 2, 256, 256), F32),
        vmem((HEADS, 2, 128, 128), F32),
        vmem((HEADS, 128, 128), F32),
        vmem((HEADS, 64, 128), F32),
        vmem((HEADS, 32, 128), F32),
        vmem((HEADS, ROWS, DH), F32),
        vmem((HEADS, ROWS, DH), F32),
        vmem((HEADS, ROWS, DH), F32),
        vmem((HEADS, LEVELS, TOK, DH), F32),
        vmem((HEADS, TOK, DH), F32),
        vmem((TOK, WID), BF),
        vmem((TOK, WID), BF),
        vmem((WID, TOK), BF),
        vmem((NZ, TOK, WID), BF),
        vmem((NZ, WID, WID), BF),
        vmem((TOK, WID), F32),
        vmem((TOK, WID), BF),
        vmem((4, HALF, DH), F32),
        vmem((2, 2, WID, DH), F32),
        vmem((NZ, 2, WID, DH), BF),
        vmem((NZ, 2, WID, DH), BF),
        vmem((CHIPS, WID, DH), BF),
        vmem((4, 4, WID, DH), BF),
        vmem((4, WID, DH), F32),
        vmem((4, WID, DH), BF),
        vmem((4, WID, DH), BF),
        vmem((2, 7, HALF, WID), BF),
        vmem((2, 7, HALF, WID), BF),
        vmem((2, HALF, WID), F32),
        vmem((3, 2, 128, WID), BF),
        vmem((2, 128, WID), BF),
        vmem((2, 2, 64, WID), BF),
        vmem((4, 2, 32, WID), BF),
        vmem((8, DH), F32),
        vmem((8, DH), F32),
        vmem((2, 8, DH), F32),
        vmem((2, 4, 8, DH), F32),
        dma((3,)), dma((NZ,)), dma,
        dma((2, 7)), dma((2, 7)),
        dma((8,)), dma((7,)), dma((8,)), dma((7,)),
        dma((NZ,)), dma((NZ,)), dma((CHIPS,)), dma((4, 4)), dma((4,)), dma((4,)),
        dma((2, 7)), dma((2, 7)),
        dma, dma, dma((2, 4)), dma((2, 4)),
    ]
    outs = pl.pallas_call(
        kernel,
        out_shape=tuple(vmem((TOK, WID), F32) for _ in range(4))
        + (vmem((WID, DH), F32), vmem((HEADS, LEVELS), F32)),
        in_specs=[pl.BlockSpec(memory_space=pl.ANY)] * 5,
        out_specs=[pl.BlockSpec(memory_space=pltpu.VMEM)] * 6,
        scratch_shapes=scratch,
        compiler_params=pltpu.CompilerParams(
            collective_id=0, has_side_effects=True, vmem_limit_bytes=56000000
        ),
        name="layer",
    )(query_input, key_input, value_input, out_weight, out_cotangent)
    held = [pltpu.with_memory_space_constraint(x, pltpu.VMEM) for x in outs]
    anywhere = pl.BlockSpec(memory_space=pl.ANY)
    local = pl.BlockSpec(memory_space=pltpu.VMEM)
    wide = jax.ShapeDtypeStruct((TOK, WID), F32)
    outs = pl.pallas_call(
        finish,
        out_shape=(
            wide, wide, wide, wide,
            jax.ShapeDtypeStruct((WID, DH), F32),
            jax.ShapeDtypeStruct((HEADS, LEVELS), F32),
        ),
        in_specs=[local] * 6,
        out_specs=[anywhere] * 6,
        scratch_shapes=[dma((18,))],
        compiler_params=pltpu.CompilerParams(vmem_limit_bytes=1000000),
        name="finish",
    )(*held)
    return outs[:5] + (outs[5].T,)


def solution(mesh):
    in_specs = (
        P("ctx", "head"),
        P("ctx", "head"),
        P("ctx", "head"),
        P("head", None),
        P("ctx", "head"),
    )
    out_specs = (
        P("ctx", "head"),
        P("ctx", "head"),
        P("ctx", "head"),
        P("ctx", "head"),
        P("head", "ctx"),
        P(None, "head"),
    )
    return jax.shard_map(
        per_device, mesh=mesh, in_specs=in_specs, out_specs=out_specs, check_vma=False
    )
```
